32 devices in a mesh: dp: 8 (over z, y), tm: 4 (over x, core).
Axes of the slice: x: 2, y: 2, z: 4, core: 2. Of those that a mesh axis runs over, the one named last changes fastest.
Arguments:
- currents: bfloat16 [8, 32, 128, 1280], P('dp', 'tm'), may hold values from -4 to 4, as said below
- mixing: float32 [32, 32], replicated, may hold values from -1 to 1, as said below
- threshold: float32 [32], replicated, may hold values from -4 to 4, as said below
- weight: bfloat16 [1280, 1280], replicated, may hold values from -0.15625 to 0.15625
- bias: float32 [1280], replicated, may hold values from -3 to 3
- cotangent: bfloat16 [8, 32, 128, 1280], P('dp', 'tm'), may hold values from -6 to 6
Outputs:
- output: bfloat16 [8, 32, 128, 1280], P('dp', 'tm')
- current_grad: bfloat16 [8, 32, 128, 1280], P('dp', 'tm')
- weight_grad: bfloat16 [1280, 1280], P(('dp', 'tm'))
- mixing_grad: float32 [32, 32], replicated
- threshold_grad: float32 [32], replicated
- bias_grad: float32 [1280], replicated
The draws below stay inside these ranges and needn't reach their ends.
Inputs may be any that keep to these rules, and one draw needn't show every extreme that they name: `currents`: every entry is a multiple of 1/16. `mixing`: every entry is a multiple of 1/16. threshold: every entry is an odd multiple of 1/512, so that every membrane value (a multiple of 1/256) lies at least 1/512 from its threshold.
All inputs are finite; a program needn't handle non-finite values.
Results may differ from the reference program's by a relative error of at most 0.0049.
Values may be sent and summed in bfloat16 or wider, within the bound.
No kernel may reach another device: no remote copies, remote signals or barrier semaphores. Data moves between devices by JAX's collectives and lax.ppermute only.
A program may use at most 128 MiB of HBM per device.

```python
import jax
import jax.numpy as jnp
from jax import lax

D = 1280
T_STEPS = 32
TOK = 128
IMAGES = 8


def draw_currents(key, part):
    levels = jax.random.randint(key, (IMAGES, T_STEPS, TOK, D), -64, 65)
    return (levels.astype(jnp.float32) / 16.0).astype(jnp.bfloat16)


def draw_mixing(key, part):
    levels = jax.random.randint(key, (T_STEPS, T_STEPS), -16, 17)
    return levels.astype(jnp.float32) / 16.0


def draw_threshold(key, part):
    levels = jax.random.randint(key, (T_STEPS,), -1024, 1024)
    return (2 * levels + 1).astype(jnp.float32) / 512.0


def level_of(own_key, dims, pieces, least, largest):
    loudness = 1.0
    for axis_at, parts in pieces:
        draws = jax.random.uniform(jax.random.fold_in(jax.random.fold_in(own_key, 6), axis_at), (parts,), jnp.float32, least / len(pieces), largest / len(pieces))
        loudness = loudness * jnp.repeat(jnp.exp(draws), dims[axis_at] // parts).reshape((-1,) + (1,) * (len(dims) - 1 - axis_at))
    return loudness


def scatter_about(stream_key, dims, scale, most, cuts=(), held_as=jnp.bfloat16):
    drawn = scale * jax.random.normal(stream_key, dims, jnp.float32)
    if cuts:
        drawn = drawn * level_of(stream_key, dims, cuts, -0.22, 0.18)
    return jnp.clip(drawn, -most, most).astype(held_as)


def setup_inputs(seed: int = 0) -> dict:
    key_list = jax.random.split(jax.random.key(seed), 7)
    return {
        "currents": draw_currents(jax.random.fold_in(key_list[6], 71), 0),
        "mixing": draw_mixing(jax.random.fold_in(key_list[6], 71), 0),
        "threshold": draw_threshold(jax.random.fold_in(key_list[6], 71), 0),
        "weight": scatter_about(key_list[3], (D, D), D ** -0.5, 0.15625),
        "bias": scatter_about(key_list[4], (D,), 0.5, 3.0, (), jnp.float32),
        "cotangent": scatter_about(key_list[5], (IMAGES, T_STEPS, TOK, D), 1.0, 6.0, ((0, 8), (1, 4))),
    }


def reference(currents, mixing, threshold, weight, bias, cotangent):
    highest = lax.Precision.HIGHEST
    shape = currents.shape
    width = shape[3]
    wide_cur = currents.astype(jnp.float32)
    membrane = jnp.einsum('tj,ijnd->itnd', mixing, wide_cur, precision=highest)
    shifted = membrane - threshold[None, :, None, None]
    spikes = (shifted > 0).astype(jnp.bfloat16)
    spike_rows = spikes.reshape(-1, width)
    grad_rows = cotangent.reshape(-1, width)
    output = (jnp.dot(spike_rows, weight, preferred_element_type=jnp.float32) + bias).astype(jnp.bfloat16)
    sigmoid_val = jax.nn.sigmoid(shifted)
    surrogate = sigmoid_val * (1.0 - sigmoid_val)
    spike_grad = jnp.einsum('re,de->rd', grad_rows, weight, preferred_element_type=jnp.float32).astype(jnp.bfloat16)
    membrane_grad = spike_grad.reshape(shape).astype(jnp.float32) * surrogate
    current_grad = jnp.einsum('tj,itnd->ijnd', mixing, membrane_grad, precision=highest).astype(jnp.bfloat16)
    weight_grad = jnp.einsum('rd,re->de', spike_rows, grad_rows, preferred_element_type=jnp.float32).astype(jnp.bfloat16)
    mixing_grad = jnp.einsum('itnd,ijnd->tj', membrane_grad, wide_cur, precision=highest)
    threshold_grad = -jnp.sum(membrane_grad, axis=(0, 2, 3))
    bias_grad = jnp.sum(grad_rows.astype(jnp.float32), axis=0)
    return (output.reshape(shape), current_grad, weight_grad, mixing_grad, threshold_grad, bias_grad)
```

```python
import functools

import jax
import jax.numpy as jnp
from jax import lax
from jax.experimental import pallas as pl
from jax.experimental.pallas import tpu as pltpu
from jax.sharding import PartitionSpec as P

GROUP = 16
CHUNKS = (32, 32, 32, 32)


def xor_permute(value, axis, size, mask):
    return lax.ppermute(value, axis, [(i, i ^ mask) for i in range(size)])


def forward_kernel(parts, kron_ref, thr_ref, sg_ref, *refs):
    sources = refs[:parts]
    spikes_ref, mg_ref, cross_ref, tsum_ref = refs[-4:]
    steps, group, width = mg_ref.shape
    rows = steps * group

    @pl.when(pl.program_id(0) == 0)
    def _():
        cross_ref[...] = jnp.zeros_like(cross_ref)
        tsum_ref[...] = jnp.zeros_like(tsum_ref)

    kron = kron_ref[...]
    thr = thr_ref[...]
    tile = 256
    for at in range(0, width, tile):
        cur = jnp.concatenate(
            [s[:, :, at : at + tile].reshape(rows, tile) for s in sources], axis=0
        )
        membrane = jnp.dot(kron, cur, preferred_element_type=jnp.float32)
        shifted = membrane - thr
        spikes_ref[:, :, at : at + tile] = (
            jnp.where(shifted > 0, 1.0, 0.0).astype(jnp.bfloat16).reshape(steps, group, tile)
        )
        small = jnp.exp(-jnp.abs(shifted))
        part = 1.0 / (1.0 + small)
        surrogate = small * part * part
        sg = sg_ref[:, :, at : at + tile].reshape(rows, tile).astype(jnp.float32)
        mg = sg * surrogate
        high = mg.astype(jnp.bfloat16)
        low = (mg - high.astype(jnp.float32)).astype(jnp.bfloat16)
        mg_ref[:, :, at : at + tile] = high.reshape(steps, group, tile)
        contract = (((1,), (1,)), ((), ()))
        cross_ref[...] += lax.dot_general(
            high, cur, contract, preferred_element_type=jnp.float32
        ) + lax.dot_general(low, cur, contract, preferred_element_type=jnp.float32)
        total = mg[:, :128]
        for piece in range(128, tile, 128):
            total = total + mg[:, piece : piece + 128]
        tsum_ref[...] += total


def backward_kernel(parts, kron_ref, *refs):
    sources = refs[:parts]
    out_ref = refs[-1]
    steps, group, width = out_ref.shape
    rows = steps * group
    kron = kron_ref[...]
    tile = 256
    for at in range(0, width, tile):
        mg = jnp.concatenate(
            [s[:, :, at : at + tile].reshape(rows, tile) for s in sources], axis=0
        )
        grad = jnp.dot(kron, mg, preferred_element_type=jnp.float32)
        out_ref[:, :, at : at + tile] = grad.astype(jnp.bfloat16).reshape(steps, group, tile)


def forward_chunk(start, size, kron, thr, spike_grad, sources, spikes):
    steps, tokens, width = spike_grad.shape
    parts = len(sources)
    rows = steps * GROUP
    first = start // GROUP
    whole = pl.BlockSpec((steps, GROUP, width), lambda g: (0, g + first, 0))
    piece = pl.BlockSpec((steps, GROUP, width), lambda g: (0, g, 0))
    fixed = lambda shape: pl.BlockSpec(shape, lambda g: (0, 0))
    args = [kron, thr, spike_grad, *sources]
    specs = [fixed(kron.shape), fixed(thr.shape), whole, whole, whole] + [piece] * (parts - 2)
    aliases = {}
    if spikes is not None:
        aliases = {len(args): 0}
        args.append(spikes)
        specs.append(pl.BlockSpec(memory_space=pl.ANY))
    return pl.pallas_call(
        functools.partial(forward_kernel, parts),
        grid=(size // GROUP,),
        in_specs=specs,
        out_specs=(whole, piece, fixed((rows, parts * rows)), fixed((rows, 128))),
        out_shape=(
            jax.ShapeDtypeStruct((steps, tokens, width), jnp.bfloat16),
            jax.ShapeDtypeStruct((steps, size, width), jnp.bfloat16),
            jax.ShapeDtypeStruct((rows, parts * rows), jnp.float32),
            jax.ShapeDtypeStruct((rows, 128), jnp.float32),
        ),
        input_output_aliases=aliases,
        cost_estimate=pl.CostEstimate(
            flops=6 * rows * parts * rows * width * (size // GROUP),
            bytes_accessed=2 * (parts + 3) * steps * size * width,
            transcendentals=2 * steps * size * width,
        ),
        name="forward_chunk",
    )(*args)


def backward_chunk(start, kron, sources, grad, tokens):
    steps, size, width = sources[0].shape
    first = start // GROUP
    piece = pl.BlockSpec((steps, GROUP, width), lambda g: (0, g, 0))
    args = [kron, *sources]
    specs = [pl.BlockSpec(kron.shape, lambda g: (0, 0))] + [piece] * len(sources)
    aliases = {}
    if grad is not None:
        aliases = {len(args): 0}
        args.append(grad)
        specs.append(pl.BlockSpec(memory_space=pl.ANY))
    return pl.pallas_call(
        functools.partial(backward_kernel, len(sources)),
        grid=(size // GROUP,),
        in_specs=specs,
        out_specs=pl.BlockSpec((steps, GROUP, width), lambda g: (0, g + first, 0)),
        out_shape=jax.ShapeDtypeStruct((steps, tokens, width), jnp.bfloat16),
        input_output_aliases=aliases,
        cost_estimate=pl.CostEstimate(
            flops=2 * len(sources) * (steps * GROUP) ** 2 * width * (size // GROUP),
            bytes_accessed=2 * (len(sources) + 1) * steps * size * width,
            transcendentals=0,
        ),
        name="backward_chunk",
    )(*args)


def iota2(shape, dim):
    return lax.broadcasted_iota(jnp.int32, shape, dim)


def selectors(me, parts, steps):
    rows, cols, total = steps * GROUP, parts * steps * GROUP, parts * steps
    shift, depth = GROUP.bit_length() - 1, (steps * GROUP).bit_length() - 1
    own = me * steps + lax.shift_right_logical(iota2((rows, total), 0), shift)
    left = own == iota2((rows, total), 1)
    at = iota2((total, cols), 1)
    source = jnp.bitwise_xor(me, lax.shift_right_logical(at, depth))
    step = jnp.bitwise_and(lax.shift_right_logical(at, shift), steps - 1)
    right = source * steps + step == iota2((total, cols), 0)
    same = jnp.bitwise_and(iota2((rows, cols), 0), GROUP - 1) == jnp.bitwise_and(
        iota2((rows, cols), 1), GROUP - 1
    )
    return left, right, same


def kron_kernel(parts, steps, me_ref, mixing_ref, thr_ref, fwd_ref, bwd_ref, rows_ref):
    left, right, same = selectors(me_ref[0], parts, steps)
    mixing = mixing_ref[...].astype(jnp.bfloat16)
    one = lambda m: jnp.where(m, 1.0, 0.0).astype(jnp.bfloat16)
    dot = functools.partial(lax.dot_general, preferred_element_type=jnp.float32)
    for ref, dims in ((fwd_ref, (1, 0)), (bwd_ref, (1, 1))):
        first = dot(one(left), mixing, (((1,), (dims[1],)), ((), ()))).astype(jnp.bfloat16)
        wide = dot(first, one(right), (((1,), (0,)), ((), ())))
        ref[...] = jnp.where(same, wide, 0.0).astype(jnp.bfloat16)
    thr = jnp.broadcast_to(thr_ref[...], left.shape)
    rows_ref[...] = jnp.sum(jnp.where(left, thr, 0.0), axis=1, keepdims=True)


def build_krons(me, mixing, threshold, parts, steps):
    rows = steps * GROUP
    vmem = pl.BlockSpec(memory_space=pltpu.VMEM)
    wide = jax.ShapeDtypeStruct((rows, parts * rows), jnp.bfloat16)
    return pl.pallas_call(
        functools.partial(kron_kernel, parts, steps),
        in_specs=[pl.BlockSpec(memory_space=pltpu.SMEM), vmem, vmem],
        out_specs=(vmem, vmem, vmem),
        out_shape=(wide, wide, jax.ShapeDtypeStruct((rows, 1), jnp.float32)),
        name="build_krons",
    )(me.reshape(1), mixing, threshold.reshape(1, -1))


def sums_kernel(parts, steps, count, me_ref, bias_ref, *refs):
    crosses, tsums, out_ref = refs[:count], refs[count : 2 * count], refs[-1]
    left, right, same = selectors(me_ref[0], parts, steps)
    exact = functools.partial(
        lax.dot_general, precision=lax.Precision.HIGHEST, preferred_element_type=jnp.float32
    )
    one = lambda m: jnp.where(m, 1.0, 0.0)
    cross, tsum = crosses[0][...], tsums[0][...]
    for c, t in zip(crosses[1:], tsums[1:]):
        cross, tsum = cross + c[...], tsum + t[...]
    cross = jnp.where(same, cross, 0.0)
    narrow = exact(cross, one(right), (((1,), (1,)), ((), ())))
    total = parts * steps
    lane = iota2((narrow.shape[0], 128), 1)
    row_sum = -jnp.sum(tsum, axis=1, keepdims=True)
    block = jnp.concatenate(
        [narrow, jnp.zeros((narrow.shape[0], 128 - total), jnp.float32)], axis=1
    ) + jnp.where(lane == total, row_sum, 0.0)
    out_ref[:total, :] = exact(one(left), block, (((0,), (0,)), ((), ())))
    out_ref[total:, :] = bias_ref[...]


def pack_sums(me, bias_rows, crosses, tsums, parts, steps):
    vmem = pl.BlockSpec(memory_space=pltpu.VMEM)
    rows = parts * steps + bias_rows.shape[0]
    return pl.pallas_call(
        functools.partial(sums_kernel, parts, steps, len(crosses)),
        in_specs=[pl.BlockSpec(memory_space=pltpu.SMEM)] + [vmem] * (1 + 2 * len(crosses)),
        out_specs=vmem,
        out_shape=jax.ShapeDtypeStruct((rows, 128), jnp.float32),
        name="pack_sums",
    )(me.reshape(1), bias_rows, *crosses, *tsums)


def after(value, *earlier):
    return lax.optimization_barrier((value, *earlier))[0]


def body(ndp, ntm, currents, mixing, threshold, weight, bias, cotangent):
    _, steps, tokens, width = currents.shape
    me = lax.axis_index("tm")
    bits = lambda n: n.bit_length() - 1
    own = currents[0]
    spans = [(sum(CHUNKS[:i]), n) for i, n in enumerate(CHUNKS)]
    far = range(2, ntm, 2)

    cuts = [own[:, s : s + n] for s, n in spans]
    across = [[xor_permute(cut, "tm", ntm, k) for k in far] for cut in cuts]
    sibling = xor_permute(own, "tm", ntm, 1)
    kron_fwd, kron_bwd, thr_rows = build_krons(me, mixing, threshold, ntm, steps)

    grad_rows = cotangent.reshape(-1, width)
    spike_grad = (
        jnp.einsum("re,de->rd", grad_rows, weight, preferred_element_type=jnp.float32)
        .astype(jnp.bfloat16)
        .reshape(steps, tokens, width)
    )
    bias_term = jnp.sum(grad_rows.astype(jnp.float32), axis=0)

    def pass_on(values, token):
        found = []
        for value in values:
            value = after(value, token)
            found += [value, xor_permute(value, "tm", ntm, 1)]
        return found

    spikes, token = None, spike_grad
    crosses, tsums, mgs, mg_across, mg_sibling = [], [], [], [], []
    for (s, n), got in zip(spans, across):
        spikes, mg, cross, tsum = forward_chunk(
            s, n, kron_fwd, thr_rows, spike_grad, [own, sibling] + pass_on(got, token), spikes
        )
        token = tsum
        crosses.append(cross)
        tsums.append(tsum)
        mgs.append(mg)
        mg_across.append([xor_permute(mg, "tm", ntm, k) for k in far])
        mg_sibling.append(xor_permute(mg, "tm", ntm, 1))

    spike_rows = spikes.reshape(-1, width)
    weight_term = jnp.einsum("rd,re->de", spike_rows, grad_rows, preferred_element_type=jnp.float32)
    sums = pack_sums(me, bias_term.reshape(-1, 128), crosses, tsums, ntm, steps)

    bdp, btm = bits(ndp), bits(ntm)
    shard = width // (ndp * ntm)
    names = [("dp", b) for b in range(bdp - 1, -1, -1)] + [("tm", b) for b in range(btm - 1, -1, -1)]
    sizes = {"dp": ndp, "tm": ntm}
    y, zs, xs = ("dp", 0), [("dp", b) for b in range(1, bdp)], [("tm", b) for b in range(1, btm)]

    def halve(value, left, bit, dtype):
        axis, b = bit
        place = left.index(bit)
        beta = (lax.axis_index(axis) >> b) & 1
        keep = lax.dynamic_index_in_dim(value, beta, place, keepdims=False)
        send = lax.dynamic_index_in_dim(value, 1 - beta, place, keepdims=False)
        got = xor_permute(send.astype(dtype), axis, sizes[axis], 1 << b)
        return keep + got.astype(jnp.float32), [x for x in left if x != bit]

    value = weight_term.reshape((2,) * (bdp + btm) + (shard, width))
    value, left = halve(value, names, ("tm", 0), jnp.float32)
    half = width // 2
    done = []
    for part, route in ((value[..., :half], [y] + zs), (value[..., half:], zs + [y])):
        rest = left
        for bit in route:
            part, rest = halve(part, rest, bit, jnp.bfloat16)
        done.append(part)
    value = jnp.concatenate(done, axis=-1)
    for bit in xs:
        value, rest = halve(value, rest, bit, jnp.bfloat16)
    weight_grad = value.astype(jnp.bfloat16)

    for axis, b in [("tm", 0), y] + zs + xs:
        sums = sums + xor_permute(sums, axis, sizes[axis], 1 << b)
    total = ntm * steps
    mixing_grad, threshold_grad = sums[:total, :total], sums[:total, total]
    bias_grad = sums[total:].reshape(-1)

    output = (
        (jnp.dot(spike_rows, weight, preferred_element_type=jnp.float32) + bias)
        .astype(jnp.bfloat16)
        .reshape(cotangent.shape)
    )

    grad, token = None, output
    for (s, n), mg, got, near in zip(spans, mgs, mg_across, mg_sibling):
        grad = backward_chunk(s, kron_bwd, [mg, near] + pass_on(got, token), grad, tokens)
        token = output
    return (output, grad[None], weight_grad, mixing_grad, threshold_grad, bias_grad)


def solution(mesh):
    return jax.shard_map(
        functools.partial(body, mesh.shape["dp"], mesh.shape["tm"]),
        mesh=mesh,
        in_specs=(P("dp", "tm", None, None), P(), P(), P(), P(), P("dp", "tm", None, None)),
        out_specs=(
            P("dp", "tm", None, None),
            P("dp", "tm", None, None),
            P(("dp", "tm"), None),
            P(),
            P(),
            P(),
        ),
        check_vma=False,
    )
```

```python
import functools

import jax
import jax.numpy as jnp
from jax import lax
from jax.experimental import pallas as pl
from jax.experimental.pallas import tpu as pltpu
from jax.sharding import PartitionSpec as P

GROUP = 16
SMALL = pl.CostEstimate(flops=1000, bytes_accessed=1000, transcendentals=0)
SMEM = pl.BlockSpec(memory_space=pltpu.SMEM)
VMEM = pl.BlockSpec(memory_space=pltpu.VMEM)


def xor_permute(value, axis, size, mask):
    return lax.ppermute(value, axis, [(i, i ^ mask) for i in range(size)])


def after(value, *earlier):
    return lax.optimization_barrier((value, *earlier))[0]


def iota2(shape, dim):
    return lax.broadcasted_iota(jnp.int32, shape, dim)


def selector(me, parts, steps):
    rows, total = parts * steps * GROUP, parts * steps
    depth, shift = (steps * GROUP).bit_length() - 1, GROUP.bit_length() - 1
    at = iota2((rows, total), 0)
    source = jnp.bitwise_xor(me, lax.shift_right_logical(at, depth))
    step = jnp.bitwise_and(lax.shift_right_logical(at, shift), steps - 1)
    return source * steps + step == iota2((rows, total), 1)


def same_token(rows):
    low = lambda dim: jnp.bitwise_and(iota2((rows, rows), dim), GROUP - 1)
    return low(0) == low(1)


def kron_kernel(parts, steps, me_ref, mixing_ref, thr_ref, fwd_ref, bwd_ref, rows_ref):
    pick = selector(me_ref[0], parts, steps)
    one = jnp.where(pick, 1.0, 0.0).astype(jnp.bfloat16)
    mixing = mixing_ref[...].astype(jnp.bfloat16)
    same = same_token(pick.shape[0])
    dot = functools.partial(lax.dot_general, preferred_element_type=jnp.float32)
    for ref, dim in ((fwd_ref, 0), (bwd_ref, 1)):
        first = dot(one, mixing, (((1,), (dim,)), ((), ()))).astype(jnp.bfloat16)
        wide = dot(first, one, (((1,), (1,)), ((), ())))
        ref[...] = jnp.where(same, wide, 0.0).astype(jnp.bfloat16)
    thr = jnp.broadcast_to(thr_ref[...], pick.shape)
    rows_ref[...] = jnp.sum(jnp.where(pick, thr, 0.0), axis=1, keepdims=True)


def build_krons(info, mixing, threshold, parts, steps):
    rows = parts * steps * GROUP
    vmem = pl.BlockSpec(memory_space=pltpu.VMEM)
    wide = jax.ShapeDtypeStruct((rows, rows), jnp.bfloat16)
    return pl.pallas_call(
        functools.partial(kron_kernel, parts, steps),
        in_specs=[pl.BlockSpec(memory_space=pltpu.SMEM), vmem, vmem],
        out_specs=(vmem, vmem, vmem),
        out_shape=(wide, wide, jax.ShapeDtypeStruct((rows, 1), jnp.float32)),
        name="build_krons",
    )(info, mixing, threshold.reshape(1, -1))


def rows_of(refs, at, tile):
    return jnp.concatenate([r[:, :, at : at + tile].reshape(-1, tile) for r in refs], axis=0)


def forward_kernel(parts, kron_ref, thr_ref, *refs):
    sources, spikes, surrogate_ref = refs[:parts], refs[parts : 2 * parts], refs[-1]
    steps, group, width = sources[0].shape
    rows = steps * group
    kron = kron_ref[...]
    thr = thr_ref[...]
    tile = 256
    for at in range(0, width, tile):
        cur = rows_of(sources, at, tile)
        shifted = jnp.dot(kron, cur, preferred_element_type=jnp.float32) - thr
        fired = jnp.where(shifted > 0, 1.0, 0.0).astype(jnp.bfloat16)
        for k in range(parts):
            spikes[k][:, :, at : at + tile] = fired[k * rows : (k + 1) * rows].reshape(
                steps, group, tile
            )
        small = jnp.exp(-jnp.abs(shifted))
        part = 1.0 / (1.0 + small)
        surrogate_ref[0, :, at : at + tile] = small * part * part


def forward(kron, thr, sources):
    parts = len(sources)
    steps, tokens, width = sources[0].shape
    piece = pl.BlockSpec((steps, GROUP, width), lambda g: (0, g, 0))
    fixed = lambda shape: pl.BlockSpec(shape, lambda g: (0, 0))
    rows = parts * steps * GROUP
    found = pl.pallas_call(
        functools.partial(forward_kernel, parts),
        grid=(tokens // GROUP,),
        in_specs=[fixed(kron.shape), fixed(thr.shape)] + [piece] * parts,
        out_specs=[piece] * parts + [pl.BlockSpec((1, rows, width), lambda g: (g, 0, 0))],
        out_shape=[jax.ShapeDtypeStruct((steps, tokens, width), jnp.bfloat16)] * parts
        + [jax.ShapeDtypeStruct((tokens // GROUP, rows, width), jnp.float32)],
        name="forward",
    )(kron, thr, *sources)
    return found[:parts], found[parts]


def parts_of(mg):
    high = mg.astype(jnp.bfloat16)
    return high, (mg - high.astype(jnp.float32)).astype(jnp.bfloat16)


def backward_kernel(parts, kron_ref, surrogate_ref, *refs):
    grads, outs = refs[:parts], refs[parts:]
    steps, group, width = grads[0].shape
    rows = steps * group
    kron = kron_ref[...]
    tile = 256
    for at in range(0, width, tile):
        mg = rows_of(grads, at, tile).astype(jnp.float32) * surrogate_ref[0, :, at : at + tile]
        grad = jnp.dot(kron, mg.astype(jnp.bfloat16), preferred_element_type=jnp.float32)
        grad = grad.astype(jnp.bfloat16)
        for k in range(parts):
            outs[k][:, :, at : at + tile] = grad[k * rows : (k + 1) * rows].reshape(
                steps, group, tile
            )


def backward(kron, surrogate, grads):
    parts = len(grads)
    steps, tokens, width = grads[0].shape
    rows = parts * steps * GROUP
    piece = pl.BlockSpec((steps, GROUP, width), lambda g: (0, g, 0))
    return pl.pallas_call(
        functools.partial(backward_kernel, parts),
        grid=(tokens // GROUP,),
        in_specs=[
            pl.BlockSpec(kron.shape, lambda g: (0, 0)),
            pl.BlockSpec((1, rows, width), lambda g: (g, 0, 0)),
        ]
        + [piece] * parts,
        out_specs=[piece] * parts,
        out_shape=[jax.ShapeDtypeStruct((steps, tokens, width), jnp.bfloat16)] * parts,
        cost_estimate=pl.CostEstimate(
            flops=8 * rows * rows * width * (tokens // GROUP),
            bytes_accessed=8 * rows * width * (tokens // GROUP),
            transcendentals=0,
        ),
        name="backward",
    )(kron, surrogate, *grads)


def cross_kernel(parts, surrogate_ref, *refs):
    sources, grads, (cross_ref, tsum_ref, both_ref) = (
        refs[:parts],
        refs[parts : 2 * parts],
        refs[2 * parts :],
    )
    steps, group, width = sources[0].shape
    every = parts * steps * group

    @pl.when(pl.program_id(0) == 0)
    def _():
        cross_ref[...] = jnp.zeros_like(cross_ref)
        tsum_ref[...] = jnp.zeros_like(tsum_ref)

    tile = 256
    total = jnp.zeros((every, 128), jnp.float32)
    for at in range(0, width, tile):
        mg = rows_of(grads, at, tile).astype(jnp.float32) * surrogate_ref[0, :, at : at + tile]
        for piece in range(0, tile, 128):
            total = total + mg[:, piece : piece + 128]
        both_ref[:every, at : at + tile], both_ref[every:, at : at + tile] = parts_of(mg)
    tsum_ref[...] += total
    cross = lax.dot_general(
        both_ref[...],
        rows_of(sources, 0, width),
        (((1,), (1,)), ((), ())),
        preferred_element_type=jnp.float32,
    )
    cross_ref[...] += cross[:every] + cross[every:]


def cross_sums(surrogate, sources, grads):
    parts = len(sources)
    steps, tokens, width = sources[0].shape
    rows = parts * steps * GROUP
    piece = pl.BlockSpec((steps, GROUP, width), lambda g: (0, g, 0))
    fixed = lambda shape: pl.BlockSpec(shape, lambda g: (0, 0))
    return pl.pallas_call(
        functools.partial(cross_kernel, parts),
        grid=(tokens // GROUP,),
        in_specs=[pl.BlockSpec((1, rows, width), lambda g: (g, 0, 0))] + [piece] * (2 * parts),
        out_specs=[fixed((rows, rows)), fixed((rows, 128))],
        out_shape=[
            jax.ShapeDtypeStruct((rows, rows), jnp.float32),
            jax.ShapeDtypeStruct((rows, 128), jnp.float32),
        ],
        scratch_shapes=[pltpu.VMEM((2 * rows, width), jnp.bfloat16)],
        cost_estimate=pl.CostEstimate(
            flops=8 * rows * rows * width * (tokens // GROUP),
            bytes_accessed=8 * rows * width * (tokens // GROUP),
            transcendentals=0,
        ),
        name="cross_sums",
    )(surrogate, *sources, *grads)


def sums_kernel(parts, steps, me_ref, bias_ref, cross_ref, tsum_ref, out_ref):
    pick = selector(me_ref[0], parts, steps)
    rows, total = pick.shape
    one = jnp.where(pick, 1.0, 0.0)
    exact = functools.partial(
        lax.dot_general, precision=lax.Precision.HIGHEST, preferred_element_type=jnp.float32
    )
    turned = (((0,), (0,)), ((), ()))
    cross = jnp.where(same_token(rows), cross_ref[...], 0.0)
    narrow = exact(cross, one, (((1,), (0,)), ((), ())))
    row_sum = -jnp.sum(tsum_ref[...], axis=1, keepdims=True)
    out_ref[...] = jnp.zeros_like(out_ref)
    out_ref[:total, :total] = exact(one, narrow, turned)
    out_ref[total : total + 8, :total] = jnp.broadcast_to(
        jnp.sum(one * row_sum, axis=0, keepdims=True), (8, total)
    )
    out_ref[total + 8 : total + 8 + bias_ref.shape[0], :] = bias_ref[...]


def pack_sums(info, bias_rows, cross, tsum, parts, steps):
    rows = parts * steps + 8 + -(-bias_rows.shape[0] // 8) * 8
    return pl.pallas_call(
        functools.partial(sums_kernel, parts, steps),
        in_specs=[SMEM, VMEM, VMEM, VMEM],
        out_specs=VMEM,
        out_shape=jax.ShapeDtypeStruct((rows, 128), jnp.float32),
        cost_estimate=SMALL,
        name="pack_sums",
    )(info, bias_rows, cross, tsum)


def place_kernel(slots, info_ref, *refs):
    pieces, (whole_ref, held_ref, in_sems, out_sems) = refs[: len(slots)], refs[-4:]
    share = held_ref.shape[2]
    loads, stores = [], []
    for n, slot in enumerate(slots):
        at = pl.multiple_of(info_ref[slot] * share, share)
        loads.append(pltpu.make_async_copy(pieces[n], held_ref.at[n], in_sems.at[n]))
        stores.append(
            pltpu.make_async_copy(
                held_ref.at[n], whole_ref.at[:, pl.ds(at, share), :], out_sems.at[n]
            )
        )
    for load in loads:
        load.start()
    for load, store in zip(loads, stores):
        load.wait()
        store.start()
    for store in stores:
        store.wait()


def place(info, pieces, slots, whole, tokens):
    steps, share, width = pieces[0].shape
    args, aliases, count = list(pieces), {}, len(pieces)
    if whole is not None:
        aliases = {1 + count: 0}
        args.append(whole)
    hbm = pl.BlockSpec(memory_space=pl.ANY)
    return pl.pallas_call(
        functools.partial(place_kernel, tuple(slots)),
        in_specs=[SMEM] + [hbm] * len(args),
        out_specs=hbm,
        out_shape=jax.ShapeDtypeStruct((steps, tokens, width), jnp.bfloat16),
        scratch_shapes=[
            pltpu.VMEM((count, steps, share, width), jnp.bfloat16),
            pltpu.SemaphoreType.DMA((count,)),
            pltpu.SemaphoreType.DMA((count,)),
        ],
        input_output_aliases=aliases,
        cost_estimate=SMALL,
        name="place",
    )(info, *args)


def combine_kernel(shapes, counts, extra, joined, info_ref, *refs):
    halves = len(shapes)
    keeps, refs = refs[:halves], refs[halves:]
    gots = []
    for count in counts:
        gots.append(refs[:count])
        refs = refs[count:]
    adds, outs = refs[:extra], refs[extra:]
    for h, (before, behind, slot) in enumerate(shapes):
        keep_ref = keeps[h]
        stay_ref, send_ref = (outs[0], outs[1]) if joined else (outs[2 * h], outs[2 * h + 1])
        beta = info_ref[slot]
        each = keep_ref.shape[0] // counts[h]
        cols = slice(h * keep_ref.shape[2], (h + 1) * keep_ref.shape[2]) if joined else slice(None)

        def value(p, b, q):
            at = (p * 2 + b) * behind + q
            if counts[h] == 1:
                got = gots[h][0][at]
            else:
                part = (p * 2 * behind) // each
                got = gots[h][part][at - part * each]
            return keep_ref[at] + got.astype(jnp.float32)

        for p in range(before):
            for q in range(behind):
                stay_ref[p * behind + q, :, cols] = value(p, beta, q)
                send_ref[p * behind + q, :, cols] = value(p, 1 - beta, q).astype(send_ref.dtype)
    if extra:
        total = adds[0][...]
        for ref in adds[1:]:
            total = total + ref[...]
        outs[-1][...] = total


def combine(info, shapes, halves, adds=(), joined=False):
    out = []
    for (keep, _), (before, behind, _) in zip(halves[:1] if joined else halves, shapes):
        cols = keep.shape[2] * (len(halves) if joined else 1)
        shape = (before * behind, keep.shape[1], cols)
        out += [
            jax.ShapeDtypeStruct(shape, jnp.float32),
            jax.ShapeDtypeStruct(shape, jnp.bfloat16),
        ]
    if adds:
        out.append(jax.ShapeDtypeStruct(adds[0].shape, jnp.float32))
    args = [k for k, _ in halves] + [g for _, got in halves for g in got] + list(adds)
    counts = tuple(len(got) for _, got in halves)
    found = pl.pallas_call(
        functools.partial(combine_kernel, tuple(shapes), counts, len(adds), joined),
        in_specs=[SMEM] + [VMEM] * len(args),
        out_specs=[VMEM] * len(out),
        out_shape=out,
        cost_estimate=SMALL,
        name="combine",
    )(info, *args)
    pairs = [(found[n], found[n + 1]) for n in range(0, len(out) - len(out) % 2, 2)]
    return pairs, found[-1]


def final_kernel(total, biases, keep_ref, got_ref, *refs):
    sums_refs, (out_ref, mix_ref, thr_ref, bias_ref) = refs[:-4], refs[-4:]
    out_ref[...] = (keep_ref[...] + got_ref[...].astype(jnp.float32)).astype(jnp.bfloat16)
    sums = sums_refs[0][...]
    for ref in sums_refs[1:]:
        sums = sums + ref[...]
    mix_ref[...] = sums[:total, :total]
    thr_ref[...] = sums[total : total + 1, :total]
    bias_ref[...] = jnp.concatenate(
        [sums[total + 8 + i : total + 9 + i] for i in range(biases)], axis=1
    )


def final(keep, got, sums, total, width):
    shape = jax.ShapeDtypeStruct
    return pl.pallas_call(
        functools.partial(final_kernel, total, width // 128),
        in_specs=[VMEM] * (2 + len(sums)),
        out_specs=[VMEM] * 4,
        out_shape=[
            shape(keep.shape, jnp.bfloat16),
            shape((total, total), jnp.float32),
            shape((1, total), jnp.float32),
            shape((1, width), jnp.float32),
        ],
        cost_estimate=SMALL,
        name="final",
    )(keep, got, *sums)


def weight_kernel(shard, parts, me_ref, spikes_ref, *refs):
    cots, keep_ref, sends = refs[:parts], refs[parts], refs[parts + 1 :]
    part = jnp.dot(
        spikes_ref[...], rows_of(cots, 0, cots[0].shape[-1]), preferred_element_type=jnp.float32
    )
    core = jnp.bitwise_and(me_ref[0], 1)
    pieces = [part[at : at + shard] for at in range(0, part.shape[0], shard)]
    for mine in range(2):

        @pl.when(core == mine)
        def _():
            for k, piece in enumerate(pieces):
                if k % 2 == mine:
                    keep_ref[k // 2] = piece

    for step, send_ref in enumerate(sends):
        for mine in range(2):

            @pl.when((core == mine) & (pl.program_id(0) == step))
            def _():
                for k, piece in enumerate(pieces):
                    if k % 2 != mine:
                        send_ref[k // 2] = piece.astype(send_ref.dtype)


def weight_half(info, turned, cots, part, shard):
    steps, tokens, width = cots[0].shape
    block, cols = width // 2, width // 2
    count = block // shard // 2
    send = jax.ShapeDtypeStruct((count, shard, cols), jnp.bfloat16)
    found = pl.pallas_call(
        functools.partial(weight_kernel, shard, len(cots)),
        grid=(2,),
        in_specs=[SMEM]
        + [pl.BlockSpec((block, turned.shape[1]), lambda i: (i, 0))]
        + [pl.BlockSpec((steps, tokens, cols), lambda i: (0, 0, part))] * len(cots),
        out_specs=[pl.BlockSpec((count, shard, cols), lambda i: (i, 0, 0))]
        + [pl.BlockSpec((count, shard, cols), lambda i: (0, 0, 0))] * 2,
        out_shape=[jax.ShapeDtypeStruct((2 * count, shard, cols), jnp.float32), send, send],
        cost_estimate=SMALL,
        name="weight_half",
    )(info, turned, *cots)
    return found[0], found[1:]


def body(ndp, ntm, currents, mixing, threshold, weight, bias, cotangent):
    _, steps, tokens, width = currents.shape
    me = lax.axis_index("tm")
    bits = lambda n: n.bit_length() - 1
    share = tokens // ntm
    bdp, btm = bits(ndp), bits(ntm)
    names = [("dp", b) for b in range(bdp - 1, -1, -1)] + [("tm", b) for b in range(btm - 1, -1, -1)]
    sizes = {"dp": ndp, "tm": ntm}
    info = jnp.stack(
        [me]
        + [(lax.axis_index(axis) >> b) & 1 for axis, b in names]
        + [me ^ k for k in range(ntm)]
    )
    slot = lambda bit: 1 + names.index(bit)
    spot = lambda k: 1 + len(names) + k

    def exchange(pieces):
        return [pieces[0]] + [xor_permute(pieces[k], "tm", ntm, k) for k in range(1, ntm)]

    def cut(value):
        found = {}
        for k in list(range(2, ntm)) + [1, 0]:
            found[k] = lax.dynamic_slice_in_dim(value, (me ^ k) * share, share, axis=1)
            value = after(value, found[k])
        return [found[k] for k in range(ntm)]

    def join(ks, pieces, whole=None):
        return place(info, pieces, [spot(k) for k in ks], whole, tokens)

    flat = lambda value: value.reshape(-1, width)
    pieces = cut(currents[0])
    currents_in = exchange(pieces)
    cots = exchange(cut(after(cotangent[0], *pieces[1:])))
    kron_fwd, kron_bwd, thr_rows = build_krons(info, mixing, threshold, ntm, steps)

    def spike_grad(cot):
        grad = jnp.einsum("re,de->rd", flat(cot), weight, preferred_element_type=jnp.float32)
        return grad.astype(jnp.bfloat16).reshape(cot.shape)

    bias_term = jnp.sum(flat(cotangent).astype(jnp.float32), axis=0)
    grads = [spike_grad(cot) for cot in cots[:2]]
    spikes, surrogate = forward(kron_fwd, after(thr_rows, bias_term, *grads), currents_in)
    outs = [
        (jnp.dot(flat(spikes[k]), weight, preferred_element_type=jnp.float32) + bias)
        .astype(jnp.bfloat16)
        .reshape(steps, share, width)
        for k in range(ntm)
    ]
    outs_in = exchange(outs)
    grads.append(None)
    grads += [spike_grad(after(cot, *outs)) for cot in cots[3:]]

    shard = width // (ndp * ntm)
    core, y = ("tm", 0), ("dp", 0)
    zs, xs = [("dp", b) for b in range(1, bdp)], [("tm", b) for b in range(1, btm)]
    half = width // 2
    left = names[:-1]

    if shard % 8 == 0:
        turned = jnp.concatenate([flat(after(a, *outs)) for a in spikes]).T
        late = cots[:2] + [after(cots[2], turned, *grads[3:])] + cots[3:]
        halves = [weight_half(info, turned, late, part, shard) for part in range(2)]
    else:
        whole = sum(
            jnp.einsum("rd,re->de", flat(a), flat(b), preferred_element_type=jnp.float32)
            for a, b in zip(spikes, cots)
        ).reshape(-1, 2, shard, width)
        pick = lambda b: lax.dynamic_index_in_dim(whole, b, 1, keepdims=False)
        keep, send = pick(me & 1), pick(1 - (me & 1)).astype(jnp.bfloat16)
        halves = [(keep[..., c : c + half], [send[..., c : c + half]]) for c in (0, half)]

    sent = halves[-1][1][0]
    routes = ([y] + zs, zs + [y])

    def go(value, *path):
        if all(axis == path[0][0] for axis, _ in path):
            axis = path[0][0]
            return xor_permute(value, axis, sizes[axis], sum(1 << b for _, b in path))
        mask = sum((1 << b) * (ntm if axis == "dp" else 1) for axis, b in path)
        return xor_permute(value, ("dp", "tm"), ndp * ntm, mask)

    def step(state, lefts, bits, adds=(), joined=False):
        shapes = []
        for rest, bit in zip(lefts, bits):
            p = rest.index(bit)
            shapes.append((1 << p, 1 << (len(rest) - p - 1), slot(bit)))
        pairs, total = combine(info, shapes, state, adds, joined)
        return pairs, [[x for x in rest if x != bit] for rest, bit in zip(lefts, bits)], total

    def travel(pairs, bits):
        return [(keep, [go(send, bit)]) for (keep, send), bit in zip(pairs, bits)]

    state = [(keep, [go(after(send, sent), core) for send in sends]) for keep, sends in halves]
    bits = [route[0] for route in routes]
    pairs, lefts, _ = step(state, [left, left], bits)
    state = travel(pairs, bits)
    grads[2] = spike_grad(after(cots[2], outs_in[-1], *[send for _, send in pairs]))
    cgrads = list(backward(kron_bwd, surrogate, grads))
    cgrads_in = exchange(cgrads)

    for at in range(1, bdp):
        gate, adds = [], ()
        if at == 1:
            gate = outs_in[2:-1] + cgrads
        elif at == 2:
            gate = [sums]
        elif at == 3:
            adds = few
        else:
            adds = [total, go(total, ("dp", at - 2))]
        if gate:
            state[0] = (after(state[0][0], *gate), state[0][1])
        bits = [route[at] for route in routes]
        pairs, lefts, total = step(state, lefts, bits, adds)
        state = travel(pairs, bits)
        sends = [send for _, send in pairs]
        if at == 1:
            gated = after(surrogate, *sends)
            cross, tsum = cross_sums(gated, currents_in, grads)
            sums = pack_sums(info, bias_term.reshape(-1, 128), cross, tsum, ntm, steps)
        if at == 2:
            sums = after(sums, *sends)
            sums = sums + go(sums, core)
            few = [sums, go(sums, y), go(sums, ("dp", 1)), go(sums, y, ("dp", 1))]
    adds = few if bdp == 3 else [total, go(total, ("dp", bdp - 2))]
    early = [k for k in range(ntm) if k != 2]
    current_grad = join(early, [after(cgrads_in[0], *sends)] + [cgrads_in[k] for k in early[1:]])
    state[0] = (after(state[0][0], current_grad), state[0][1])
    current_grad = join([2], [cgrads_in[2]], current_grad)

    pairs, lefts, total = step(state, lefts, [xs[0]] * 2, adds, joined=True)
    keep, send = pairs[0]
    output = join(range(ntm), [after(outs_in[0], send)] + outs_in[1:])
    got = go(send, xs[0])
    rest = lefts[0]
    for bit in xs[1:]:
        pairs, (rest,), _ = step([(keep, [got])], [rest], [bit])
        keep, send = pairs[0]
        got = go(send, bit)
    last = [("dp", bdp - 1)] + xs
    sums = [total]
    for n in range(1, 1 << len(last)):
        sums.append(go(total, *[bit for i, bit in enumerate(last) if n >> i & 1]))
    weight_grad, mixing_grad, threshold_grad, bias_grad = final(
        keep.reshape(shard, width), got.reshape(shard, width), sums, ntm * steps, width
    )
    return (
        output[None],
        current_grad[None],
        weight_grad,
        mixing_grad,
        threshold_grad.reshape(-1),
        bias_grad.reshape(-1),
    )


def solution(mesh):
    return jax.shard_map(
        functools.partial(body, mesh.shape["dp"], mesh.shape["tm"]),
        mesh=mesh,
        in_specs=(P("dp", "tm", None, None), P(), P(), P(), P(), P("dp", "tm", None, None)),
        out_specs=(
            P("dp", "tm", None, None),
            P("dp", "tm", None, None),
            P(("dp", "tm"), None),
            P(),
            P(),
            P(),
        ),
        check_vma=False,
    )
```

```python
import functools

import jax
import jax.numpy as jnp
from jax import lax
from jax.experimental import pallas as pl
from jax.experimental.pallas import tpu as pltpu
from jax.sharding import PartitionSpec as P

GROUP = 16
SMALL = pl.CostEstimate(flops=1000, bytes_accessed=1000, transcendentals=0)
SMEM = pl.BlockSpec(memory_space=pltpu.SMEM)
VMEM = pl.BlockSpec(memory_space=pltpu.VMEM)


def xor_permute(value, axis, size, mask):
    return lax.ppermute(value, axis, [(i, i ^ mask) for i in range(size)])


def after(value, *earlier):
    return lax.optimization_barrier((value, *earlier))[0]


def iota2(shape, dim):
    return lax.broadcasted_iota(jnp.int32, shape, dim)


def selector(me, parts, steps):
    rows, total = parts * steps * GROUP, parts * steps
    depth, shift = (steps * GROUP).bit_length() - 1, GROUP.bit_length() - 1
    at = iota2((rows, total), 0)
    source = jnp.bitwise_xor(me, lax.shift_right_logical(at, depth))
    step = jnp.bitwise_and(lax.shift_right_logical(at, shift), steps - 1)
    return source * steps + step == iota2((rows, total), 1)


def same_token(rows):
    low = lambda dim: jnp.bitwise_and(iota2((rows, rows), dim), GROUP - 1)
    return low(0) == low(1)


def kron_kernel(parts, steps, me_ref, mixing_ref, thr_ref, fwd_ref, bwd_ref, rows_ref):
    pick = selector(me_ref[0], parts, steps)
    one = jnp.where(pick, 1.0, 0.0).astype(jnp.bfloat16)
    mixing = mixing_ref[...].astype(jnp.bfloat16)
    same = same_token(pick.shape[0])
    dot = functools.partial(lax.dot_general, preferred_element_type=jnp.float32)
    for ref, dim in ((fwd_ref, 0), (bwd_ref, 1)):
        first = dot(one, mixing, (((1,), (dim,)), ((), ()))).astype(jnp.bfloat16)
        wide = dot(first, one, (((1,), (1,)), ((), ())))
        ref[...] = jnp.where(same, wide, 0.0).astype(jnp.bfloat16)
    thr = jnp.broadcast_to(thr_ref[...], pick.shape)
    rows_ref[...] = jnp.sum(jnp.where(pick, thr, 0.0), axis=1, keepdims=True)


def build_krons(info, mixing, threshold, parts, steps):
    rows = parts * steps * GROUP
    vmem = pl.BlockSpec(memory_space=pltpu.VMEM)
    wide = jax.ShapeDtypeStruct((rows, rows), jnp.bfloat16)
    return pl.pallas_call(
        functools.partial(kron_kernel, parts, steps),
        in_specs=[pl.BlockSpec(memory_space=pltpu.SMEM), vmem, vmem],
        out_specs=(vmem, vmem, vmem),
        out_shape=(wide, wide, jax.ShapeDtypeStruct((rows, 1), jnp.float32)),
        name="build_krons",
    )(info, mixing, threshold.reshape(1, -1))


def rows_of(refs, at, tile):
    return jnp.concatenate([r[:, :, at : at + tile].reshape(-1, tile) for r in refs], axis=0)


def forward_kernel(parts, kron_ref, thr_ref, *refs):
    sources, spikes, surrogate_ref = refs[:parts], refs[parts : 2 * parts], refs[-1]
    steps, group, width = sources[0].shape
    rows = steps * group
    kron = kron_ref[...]
    thr = thr_ref[...]
    tile = 256
    for at in range(0, width, tile):
        cur = rows_of(sources, at, tile)
        shifted = jnp.dot(kron, cur, preferred_element_type=jnp.float32) - thr
        fired = jnp.where(shifted > 0, 1.0, 0.0).astype(jnp.bfloat16)
        for k in range(parts):
            spikes[k][:, :, at : at + tile] = fired[k * rows : (k + 1) * rows].reshape(
                steps, group, tile
            )
        small = jnp.exp(-jnp.abs(shifted))
        part = 1.0 / (1.0 + small)
        surrogate_ref[0, :, at : at + tile] = small * part * part


def forward(kron, thr, sources):
    parts = len(sources)
    steps, tokens, width = sources[0].shape
    piece = pl.BlockSpec((steps, GROUP, width), lambda g: (0, g, 0))
    fixed = lambda shape: pl.BlockSpec(shape, lambda g: (0, 0))
    rows = parts * steps * GROUP
    found = pl.pallas_call(
        functools.partial(forward_kernel, parts),
        grid=(tokens // GROUP,),
        in_specs=[fixed(kron.shape), fixed(thr.shape)] + [piece] * parts,
        out_specs=[piece] * parts + [pl.BlockSpec((1, rows, width), lambda g: (g, 0, 0))],
        out_shape=[jax.ShapeDtypeStruct((steps, tokens, width), jnp.bfloat16)] * parts
        + [jax.ShapeDtypeStruct((tokens // GROUP, rows, width), jnp.float32)],
        name="forward",
    )(kron, thr, *sources)
    return found[:parts], found[parts]


def parts_of(mg):
    high = mg.astype(jnp.bfloat16)
    return high, (mg - high.astype(jnp.float32)).astype(jnp.bfloat16)


def backward_kernel(parts, kron_ref, surrogate_ref, *refs):
    grads, outs = refs[:parts], refs[parts:]
    steps, group, width = grads[0].shape
    rows = steps * group
    kron = kron_ref[...]
    tile = 256
    for at in range(0, width, tile):
        mg = rows_of(grads, at, tile).astype(jnp.float32) * surrogate_ref[0, :, at : at + tile]
        grad = jnp.dot(kron, mg.astype(jnp.bfloat16), preferred_element_type=jnp.float32)
        grad = grad.astype(jnp.bfloat16)
        for k in range(parts):
            outs[k][:, :, at : at + tile] = grad[k * rows : (k + 1) * rows].reshape(
                steps, group, tile
            )


def backward(kron, surrogate, grads):
    parts = len(grads)
    steps, tokens, width = grads[0].shape
    rows = parts * steps * GROUP
    piece = pl.BlockSpec((steps, GROUP, width), lambda g: (0, g, 0))
    return pl.pallas_call(
        functools.partial(backward_kernel, parts),
        grid=(tokens // GROUP,),
        in_specs=[
            pl.BlockSpec(kron.shape, lambda g: (0, 0)),
            pl.BlockSpec((1, rows, width), lambda g: (g, 0, 0)),
        ]
        + [piece] * parts,
        out_specs=[piece] * parts,
        out_shape=[jax.ShapeDtypeStruct((steps, tokens, width), jnp.bfloat16)] * parts,
        cost_estimate=pl.CostEstimate(
            flops=2 * rows * rows * width * (tokens // GROUP),
            bytes_accessed=2 * rows * width * (tokens // GROUP),
            transcendentals=0,
        ),
        name="backward",
    )(kron, surrogate, *grads)


def cross_of(grads, surrogate, sources, cross_ref, tsum_ref, both_ref):
    width = sources[0].shape[-1]
    every = tsum_ref.shape[0]

    @pl.when(pl.program_id(0) == 0)
    def _():
        cross_ref[...] = jnp.zeros_like(cross_ref)
        tsum_ref[...] = jnp.zeros_like(tsum_ref)

    tile = 256
    total = jnp.zeros((every, 128), jnp.float32)
    for at in range(0, width, tile):
        mg = rows_of(grads, at, tile).astype(jnp.float32) * surrogate(at, tile)
        for piece in range(0, tile, 128):
            total = total + mg[:, piece : piece + 128]
        both_ref[:every, at : at + tile], both_ref[every:, at : at + tile] = parts_of(mg)
    tsum_ref[...] += total
    cross = lax.dot_general(
        both_ref[...],
        rows_of(sources, 0, width),
        (((1,), (1,)), ((), ())),
        preferred_element_type=jnp.float32,
    )
    cross_ref[...] += cross[:every] + cross[every:]


def early_kernel(parts, surrogate_ref, *refs):
    sources, grads, rest = refs[:parts], refs[parts : 2 * parts - 1], refs[2 * parts - 1 :]
    rows = sources[0].shape[0] * sources[0].shape[1]

    def surrogate(at, tile):
        value = surrogate_ref[0, :, at : at + tile]
        return jnp.concatenate([value[: 2 * rows], value[3 * rows :]], axis=0)

    cross_of(grads, surrogate, sources, *rest)


def early_sums(surrogate, sources, grads):
    parts = len(sources)
    steps, share, width = sources[0].shape
    rows = steps * GROUP
    every = (parts - 1) * rows
    piece = pl.BlockSpec((steps, GROUP, width), lambda g: (0, g, 0))
    fixed = lambda shape: pl.BlockSpec(shape, lambda g: (0, 0))
    return pl.pallas_call(
        functools.partial(early_kernel, parts),
        grid=(share // GROUP,),
        in_specs=[pl.BlockSpec((1, parts * rows, width), lambda g: (g, 0, 0))]
        + [piece] * (2 * parts - 1),
        out_specs=[fixed((every, parts * rows)), fixed((every, 128))],
        out_shape=[
            jax.ShapeDtypeStruct((every, parts * rows), jnp.float32),
            jax.ShapeDtypeStruct((every, 128), jnp.float32),
        ],
        scratch_shapes=[pltpu.VMEM((2 * every, width), jnp.bfloat16)],
        cost_estimate=SMALL,
        name="early_sums",
    )(surrogate, *sources, *grads)


def sums_kernel(parts, info_ref, surrogate_ref, bias_ref, early_ref, early_tsum_ref, *refs):
    sources, (grad_ref, out_ref, cross_ref, tsum_ref, both_ref) = refs[:parts], refs[parts:]
    steps, group, _ = grad_ref.shape
    cross_of(
        [grad_ref],
        lambda at, tile: surrogate_ref[0, :, at : at + tile],
        sources,
        cross_ref,
        tsum_ref,
        both_ref,
    )

    @pl.when(pl.program_id(0) == pl.num_programs(0) - 1)
    def _():
        before = 2 * steps * group
        whole = lambda early, late: jnp.concatenate(
            [early[:before], late[...], early[before:]], axis=0
        )
        pick = selector(info_ref[0], parts, steps)
        rows, total = pick.shape
        one = jnp.where(pick, 1.0, 0.0)
        exact = functools.partial(
            lax.dot_general, precision=lax.Precision.HIGHEST, preferred_element_type=jnp.float32
        )
        cross = jnp.where(same_token(rows), whole(early_ref, cross_ref), 0.0)
        narrow = exact(cross, one, (((1,), (0,)), ((), ())))
        row_sum = -jnp.sum(whole(early_tsum_ref, tsum_ref), axis=1, keepdims=True)
        out_ref[...] = jnp.zeros_like(out_ref)
        out_ref[:total, :total] = exact(one, narrow, (((0,), (0,)), ((), ())))
        out_ref[total : total + 8, :total] = jnp.broadcast_to(
            jnp.sum(one * row_sum, axis=0, keepdims=True), (8, total)
        )
        out_ref[total + 8 : total + 8 + bias_ref.shape[0], :] = bias_ref[...]


def small_sums(info, surrogate, bias_rows, early, sources, grad):
    parts = len(sources)
    steps, share, width = sources[0].shape
    rows = steps * GROUP
    piece = pl.BlockSpec((steps, GROUP, width), lambda g: (0, g, 0))
    fixed = lambda shape: pl.BlockSpec(shape, lambda g: (0, 0))
    out_rows = parts * steps + 8 + -(-bias_rows.shape[0] // 8) * 8
    return pl.pallas_call(
        functools.partial(sums_kernel, parts),
        grid=(share // GROUP,),
        in_specs=[
            SMEM,
            pl.BlockSpec((1, rows, width), lambda g: (g, 2, 0)),
            fixed(bias_rows.shape),
            fixed(early[0].shape),
            fixed(early[1].shape),
        ]
        + [piece] * (parts + 1),
        out_specs=fixed((out_rows, 128)),
        out_shape=jax.ShapeDtypeStruct((out_rows, 128), jnp.float32),
        scratch_shapes=[
            pltpu.VMEM((rows, parts * rows), jnp.float32),
            pltpu.VMEM((rows, 128), jnp.float32),
            pltpu.VMEM((2 * rows, width), jnp.bfloat16),
        ],
        cost_estimate=pl.CostEstimate(
            flops=8 * parts * parts * rows * rows * width * (share // GROUP),
            bytes_accessed=8 * parts * rows * width * (share // GROUP),
            transcendentals=0,
        ),
        name="small_sums",
    )(info, surrogate, bias_rows, *early, *sources, grad)


HBM = pl.BlockSpec(memory_space=pl.ANY)


def place_kernel(slots, info_ref, *refs):
    pieces, (whole_ref, held_ref, in_sems, out_sems) = refs[: len(slots)], refs[len(slots) :]
    share = held_ref.shape[2]
    loads, stores = [], []
    for n, slot in enumerate(slots):
        at = pl.multiple_of(info_ref[slot] * share, share)
        loads.append(pltpu.make_async_copy(pieces[n], held_ref.at[n], in_sems.at[n]))
        stores.append(
            pltpu.make_async_copy(
                held_ref.at[n], whole_ref.at[:, pl.ds(at, share), :], out_sems.at[n]
            )
        )
    for load in loads:
        load.start()
    for load, store in zip(loads, stores):
        load.wait()
        store.start()
    for store in stores:
        store.wait()


def place(info, pieces, slots, tokens):
    steps, share, width = pieces[0].shape
    count = len(pieces)
    return pl.pallas_call(
        functools.partial(place_kernel, tuple(slots)),
        in_specs=[SMEM] + [HBM] * count,
        out_specs=HBM,
        out_shape=jax.ShapeDtypeStruct((steps, tokens, width), jnp.bfloat16),
        scratch_shapes=[
            pltpu.VMEM((count, steps, share, width), jnp.bfloat16),
            pltpu.SemaphoreType.DMA((count,)),
            pltpu.SemaphoreType.DMA((count,)),
        ],
        cost_estimate=SMALL,
        name="place",
    )(info, *pieces)


def combine_kernel(shapes, counts, extra, joined, info_ref, *refs):
    halves = len(shapes)
    keeps, refs = refs[:halves], refs[halves:]
    gots = []
    for count in counts:
        gots.append(refs[:count])
        refs = refs[count:]
    adds, outs = refs[:extra], refs[extra:]
    for h, (before, behind, slot) in enumerate(shapes):
        keep_ref = keeps[h]
        stay_ref, send_ref = (outs[0], outs[1]) if joined else (outs[2 * h], outs[2 * h + 1])
        beta = info_ref[slot]
        each = keep_ref.shape[0] // counts[h]
        cols = slice(h * keep_ref.shape[2], (h + 1) * keep_ref.shape[2]) if joined else slice(None)

        def value(p, b, q):
            at = (p * 2 + b) * behind + q
            if counts[h] == 1:
                got = gots[h][0][at]
            else:
                part = (p * 2 * behind) // each
                got = gots[h][part][at - part * each]
            return keep_ref[at] + got.astype(jnp.float32)

        for p in range(before):
            for q in range(behind):
                stay_ref[p * behind + q, :, cols] = value(p, beta, q)
                send_ref[p * behind + q, :, cols] = value(p, 1 - beta, q).astype(send_ref.dtype)
    if extra:
        total = adds[0][...]
        for ref in adds[1:]:
            total = total + ref[...]
        outs[-1][...] = total


def combine(info, shapes, halves, adds=(), joined=False):
    out = []
    for (keep, _), (before, behind, _) in zip(halves[:1] if joined else halves, shapes):
        cols = keep.shape[2] * (len(halves) if joined else 1)
        shape = (before * behind, keep.shape[1], cols)
        out += [
            jax.ShapeDtypeStruct(shape, jnp.float32),
            jax.ShapeDtypeStruct(shape, jnp.bfloat16),
        ]
    if adds:
        out.append(jax.ShapeDtypeStruct(adds[0].shape, jnp.float32))
    args = [k for k, _ in halves] + [g for _, got in halves for g in got] + list(adds)
    counts = tuple(len(got) for _, got in halves)
    found = pl.pallas_call(
        functools.partial(combine_kernel, tuple(shapes), counts, len(adds), joined),
        in_specs=[SMEM] + [VMEM] * len(args),
        out_specs=[VMEM] * len(out),
        out_shape=out,
        cost_estimate=SMALL,
        name="combine",
    )(info, *args)
    pairs = [(found[n], found[n + 1]) for n in range(0, len(out) - len(out) % 2, 2)]
    return pairs, found[-1]


def final_kernel(total, biases, keep_ref, got_ref, *refs):
    sums_refs, (out_ref, mix_ref, thr_ref, bias_ref) = refs[:-4], refs[-4:]
    out_ref[...] = (keep_ref[...] + got_ref[...].astype(jnp.float32)).astype(jnp.bfloat16)
    sums = sums_refs[0][...]
    for ref in sums_refs[1:]:
        sums = sums + ref[...]
    mix_ref[...] = sums[:total, :total]
    thr_ref[...] = sums[total : total + 1, :total]
    bias_ref[...] = sums[total + 8 : total + 8 + biases]


def final(keep, got, sums, total, width):
    shape = jax.ShapeDtypeStruct
    return pl.pallas_call(
        functools.partial(final_kernel, total, width // 128),
        in_specs=[VMEM] * (2 + len(sums)),
        out_specs=[VMEM] * 4,
        out_shape=[
            shape(keep.shape, jnp.bfloat16),
            shape((total, total), jnp.float32),
            shape((1, total), jnp.float32),
            shape((width // 128, 128), jnp.float32),
        ],
        cost_estimate=SMALL,
        name="final",
    )(keep, got, *sums)


def weight_kernel(shard, parts, info_ref, *refs):
    spikes, cots, outs = refs[:parts], refs[parts : 2 * parts], refs[2 * parts :]
    part = lax.dot_general(
        rows_of(spikes, 0, spikes[0].shape[-1]),
        rows_of(cots, 0, cots[0].shape[-1]),
        (((0,), (0,)), ((), ())),
        preferred_element_type=jnp.float32,
    )
    core = jnp.bitwise_and(info_ref[0], 1)
    step = pl.program_id(0)
    pieces = [part[at : at + shard] for at in range(0, part.shape[0], shard)]
    for side in range(2):
        for mine in range(2):

            @pl.when((core == mine) & (step // 2 == side))
            def _():
                for k, piece in enumerate(pieces):
                    if k % 2 == mine:
                        outs[side][k // 2] = piece

    for at in range(4):
        for mine in range(2):

            @pl.when((core == mine) & (step == at))
            def _():
                for k, piece in enumerate(pieces):
                    if k % 2 != mine:
                        outs[2 + at][k // 2] = piece.astype(jnp.bfloat16)


def weight_halves(info, spikes, cots, shard):
    steps, tokens, width = spikes[0].shape
    block, cols = width // 2, width // 2
    count = block // shard // 2
    send = jax.ShapeDtypeStruct((count, shard, cols), jnp.bfloat16)
    keep = jax.ShapeDtypeStruct((2 * count, shard, cols), jnp.float32)
    found = pl.pallas_call(
        functools.partial(weight_kernel, shard, len(spikes)),
        grid=(4,),
        in_specs=[SMEM]
        + [pl.BlockSpec((steps, tokens, block), lambda i: (0, 0, i % 2))] * len(spikes)
        + [pl.BlockSpec((steps, tokens, cols), lambda i: (0, 0, i // 2))] * len(spikes),
        out_specs=[
            pl.BlockSpec((count, shard, cols), lambda i: (jnp.minimum(i, 1), 0, 0)),
            pl.BlockSpec((count, shard, cols), lambda i: (jnp.maximum(i - 2, 0), 0, 0)),
        ]
        + [pl.BlockSpec((count, shard, cols), lambda i: (0, 0, 0))] * 4,
        out_shape=[keep, keep] + [send] * 4,
        cost_estimate=SMALL,
        name="weight_halves",
    )(info, *spikes, *cots)
    return [(found[0], found[2:4]), (found[1], found[4:6])]


def body(ndp, ntm, currents, mixing, threshold, weight, bias, cotangent):
    _, steps, tokens, width = currents.shape
    me = lax.axis_index("tm")
    bits = lambda n: n.bit_length() - 1
    share = tokens // ntm
    bdp, btm = bits(ndp), bits(ntm)
    names = [("dp", b) for b in range(bdp - 1, -1, -1)] + [("tm", b) for b in range(btm - 1, -1, -1)]
    sizes = {"dp": ndp, "tm": ntm}
    info = jnp.stack(
        [me]
        + [(lax.axis_index(axis) >> b) & 1 for axis, b in names]
        + [me ^ k for k in range(ntm)]
    )
    slot = lambda bit: 1 + names.index(bit)
    spot = lambda k: 1 + len(names) + k

    def exchange(pieces):
        return [pieces[0]] + [xor_permute(pieces[k], "tm", ntm, k) for k in range(1, ntm)]

    def cut(value):
        found = {}
        for k in list(range(2, ntm)) + [1, 0]:
            found[k] = lax.dynamic_slice_in_dim(value, (me ^ k) * share, share, axis=1)
            value = after(value, found[k])
        return [found[k] for k in range(ntm)]

    flat = lambda value: value.reshape(-1, width)
    pieces = cut(currents[0])
    currents_in = exchange(pieces)
    cots = exchange(cut(after(cotangent[0], *pieces[1:])))
    kron_fwd, kron_bwd, thr_rows = build_krons(info, mixing, threshold, ntm, steps)

    def spike_grad(cot):
        grad = jnp.einsum("re,de->rd", flat(cot), weight, preferred_element_type=jnp.float32)
        return grad.astype(jnp.bfloat16).reshape(cot.shape)

    bias_term = jnp.sum(flat(cotangent).astype(jnp.float32), axis=0)
    grads = [spike_grad(cot) for cot in cots[:2]]
    spikes, surrogate = forward(kron_fwd, after(thr_rows, bias_term, *grads), currents_in)
    outs = [
        (jnp.dot(flat(spikes[k]), weight, preferred_element_type=jnp.float32) + bias)
        .astype(jnp.bfloat16)
        .reshape(steps, share, width)
        for k in range(ntm)
    ]
    outs_in = exchange(outs)
    grads.append(None)
    grads += [spike_grad(after(cot, *outs)) for cot in cots[3:]]

    others = [k for k in range(ntm) if k != 2]
    early = early_sums(after(surrogate, *outs), currents_in, [grads[k] for k in others])

    shard = width // (ndp * ntm)
    core, y = ("tm", 0), ("dp", 0)
    zs, xs = [("dp", b) for b in range(1, bdp)], [("tm", b) for b in range(1, btm)]
    half = width // 2
    left = names[:-1]

    if shard % 8 == 0:
        late = cots[:2] + [after(cots[2], *outs, *early)] + cots[3:]
        halves = weight_halves(info, spikes, late, shard)
    else:
        whole = sum(
            jnp.einsum("rd,re->de", flat(a), flat(b), preferred_element_type=jnp.float32)
            for a, b in zip(spikes, cots)
        ).reshape(-1, 2, shard, width)
        pick = lambda b: lax.dynamic_index_in_dim(whole, b, 1, keepdims=False)
        keep, send = pick(me & 1), pick(1 - (me & 1)).astype(jnp.bfloat16)
        halves = [(keep[..., c : c + half], [send[..., c : c + half]]) for c in (0, half)]

    sent = halves[-1][1][0]
    routes = ([y] + zs, zs + [y])

    def go(value, *path):
        if all(axis == path[0][0] for axis, _ in path):
            axis = path[0][0]
            return xor_permute(value, axis, sizes[axis], sum(1 << b for _, b in path))
        mask = sum((1 << b) * (ntm if axis == "dp" else 1) for axis, b in path)
        return xor_permute(value, ("dp", "tm"), ndp * ntm, mask)

    def step(state, lefts, bits, joined=False):
        shapes = []
        for rest, bit in zip(lefts, bits):
            p = rest.index(bit)
            shapes.append((1 << p, 1 << (len(rest) - p - 1), slot(bit)))
        pairs, _ = combine(info, shapes, state, (), joined)
        return pairs, [[x for x in rest if x != bit] for rest, bit in zip(lefts, bits)]

    def travel(pairs, bits):
        return [(keep, [go(send, bit)]) for (keep, send), bit in zip(pairs, bits)]

    state = [(keep, [go(after(send, sent), core) for send in sends]) for keep, sends in halves]
    bits = [route[0] for route in routes]
    pairs, lefts = step(state, [left, left], bits)
    state = travel(pairs, bits)
    grads[2] = spike_grad(after(cots[2], outs_in[-1], *[send for _, send in pairs]))
    cgrads = list(backward(kron_bwd, surrogate, grads))
    cgrads_in = exchange(cgrads)

    def meet(sums, *bits):
        for bit in bits:
            sums = sums + go(sums, bit)
        return sums

    for at in range(1, bdp):
        gate = outs_in[1:3] + cgrads if at == 1 else [sums]
        if at == 2:
            gate.append(cgrads_in[1])
        state[0] = (after(state[0][0], *gate), state[0][1])
        bits = [route[at] for route in routes]
        pairs, lefts = step(state, lefts, bits)
        state = travel(pairs, bits)
        sends = [send for _, send in pairs]
        if at == 1:
            sums = small_sums(
                info,
                after(surrogate, *sends),
                bias_term.reshape(-1, 128),
                early,
                currents_in,
                grads[2],
            )
            hops = [core, y] + zs
        else:
            few = 3 if at == 2 else 1
            sums = meet(after(sums, *sends), *hops[:few])
            hops = hops[few:]
    state[0] = (after(state[0][0], sums), state[0][1])

    pairs, lefts = step(state, lefts, [xs[0]] * 2, joined=True)
    keep, send = pairs[0]
    got = go(send, xs[0])
    spots = list(map(spot, range(ntm)))
    output = place(info, [after(outs_in[0], send)] + outs_in[1:], spots, tokens)
    meeting = [after(sums, send)]
    meeting.append(go(meeting[0], *hops))
    sums = after(meeting[0], output) + meeting[1]
    current_grad = place(info, [after(cgrads_in[0], sums)] + cgrads_in[1:], spots, tokens)
    rest = lefts[0]
    for bit in xs[1:]:
        pairs, (rest,) = step([(keep, [got])], [rest], [bit])
        keep, send = pairs[0]
        got = go(send, bit)
    sums = [sums] + [
        go(sums, *[bit for i, bit in enumerate(xs) if n >> i & 1]) for n in range(1, 1 << len(xs))
    ]
    weight_grad, mixing_grad, threshold_grad, bias_grad = final(
        keep.reshape(shard, width), got.reshape(shard, width), sums, ntm * steps, width
    )
    return (
        output[None],
        current_grad[None],
        weight_grad,
        mixing_grad,
        threshold_grad.reshape(-1),
        bias_grad.reshape(-1),
    )


def solution(mesh):
    return jax.shard_map(
        functools.partial(body, mesh.shape["dp"], mesh.shape["tm"]),
        mesh=mesh,
        in_specs=(P("dp", "tm", None, None), P(), P(), P(), P(), P("dp", "tm", None, None)),
        out_specs=(
            P("dp", "tm", None, None),
            P("dp", "tm", None, None),
            P(("dp", "tm"), None),
            P(),
            P(),
            P(),
        ),
        check_vma=False,
    )
```

```python
import functools

import jax
import jax.numpy as jnp
from jax import lax
from jax.experimental import pallas as pl
from jax.experimental.pallas import tpu as pltpu
from jax.sharding import PartitionSpec as P

GROUP = 16
SMALL = pl.CostEstimate(flops=1000, bytes_accessed=1000, transcendentals=0)
SMEM = pl.BlockSpec(memory_space=pltpu.SMEM)
VMEM = pl.BlockSpec(memory_space=pltpu.VMEM)


def xor_permute(value, axis, size, mask):
    return lax.ppermute(value, axis, [(i, i ^ mask) for i in range(size)])


def after(value, *earlier):
    return lax.optimization_barrier((value, *earlier))[0]


def iota2(shape, dim):
    return lax.broadcasted_iota(jnp.int32, shape, dim)


def selector(me, parts, steps):
    rows, total = parts * steps * GROUP, parts * steps
    depth, shift = (steps * GROUP).bit_length() - 1, GROUP.bit_length() - 1
    at = iota2((rows, total), 0)
    source = jnp.bitwise_xor(me, lax.shift_right_logical(at, depth))
    step = jnp.bitwise_and(lax.shift_right_logical(at, shift), steps - 1)
    return source * steps + step == iota2((rows, total), 1)


def same_token(rows):
    low = lambda dim: jnp.bitwise_and(iota2((rows, rows), dim), GROUP - 1)
    return low(0) == low(1)


def kron_kernel(parts, steps, me_ref, mixing_ref, thr_ref, fwd_ref, bwd_ref, rows_ref):
    pick = selector(me_ref[0], parts, steps)
    one = jnp.where(pick, 1.0, 0.0).astype(jnp.bfloat16)
    mixing = mixing_ref[...].astype(jnp.bfloat16)
    same = same_token(pick.shape[0])
    dot = functools.partial(lax.dot_general, preferred_element_type=jnp.float32)
    for ref, dim in ((fwd_ref, 0), (bwd_ref, 1)):
        first = dot(one, mixing, (((1,), (dim,)), ((), ()))).astype(jnp.bfloat16)
        wide = dot(first, one, (((1,), (1,)), ((), ())))
        ref[...] = jnp.where(same, wide, 0.0).astype(jnp.bfloat16)
    thr = jnp.broadcast_to(thr_ref[...], pick.shape)
    rows_ref[...] = jnp.sum(jnp.where(pick, thr, 0.0), axis=1, keepdims=True)


def build_krons(info, mixing, threshold, parts, steps):
    rows = parts * steps * GROUP
    vmem = pl.BlockSpec(memory_space=pltpu.VMEM)
    wide = jax.ShapeDtypeStruct((rows, rows), jnp.bfloat16)
    return pl.pallas_call(
        functools.partial(kron_kernel, parts, steps),
        in_specs=[pl.BlockSpec(memory_space=pltpu.SMEM), vmem, vmem],
        out_specs=(vmem, vmem, vmem),
        out_shape=(wide, wide, jax.ShapeDtypeStruct((rows, 1), jnp.float32)),
        name="build_krons",
    )(info, mixing, threshold.reshape(1, -1))


def rows_of(refs, at, tile):
    return jnp.concatenate([r[:, :, at : at + tile].reshape(-1, tile) for r in refs], axis=0)


def forward_kernel(parts, kron_ref, thr_ref, *refs):
    sources, spikes, surrogate_ref = refs[:parts], refs[parts : 2 * parts], refs[-1]
    steps, group, width = sources[0].shape
    rows = steps * group
    kron = kron_ref[...]
    thr = thr_ref[...]
    tile = 256
    for at in range(0, width, tile):
        cur = rows_of(sources, at, tile)
        shifted = jnp.dot(kron, cur, preferred_element_type=jnp.float32) - thr
        fired = jnp.where(shifted > 0, 1.0, 0.0).astype(jnp.bfloat16)
        for k in range(parts):
            spikes[k][:, :, at : at + tile] = fired[k * rows : (k + 1) * rows].reshape(
                steps, group, tile
            )
        small = jnp.exp(-jnp.abs(shifted))
        part = 1.0 / (1.0 + small)
        surrogate_ref[0, :, at : at + tile] = small * part * part


def forward(kron, thr, sources):
    parts = len(sources)
    steps, tokens, width = sources[0].shape
    piece = pl.BlockSpec((steps, GROUP, width), lambda g: (0, g, 0))
    fixed = lambda shape: pl.BlockSpec(shape, lambda g: (0, 0))
    rows = parts * steps * GROUP
    found = pl.pallas_call(
        functools.partial(forward_kernel, parts),
        grid=(tokens // GROUP,),
        in_specs=[fixed(kron.shape), fixed(thr.shape)] + [piece] * parts,
        out_specs=[piece] * parts + [pl.BlockSpec((1, rows, width), lambda g: (g, 0, 0))],
        out_shape=[jax.ShapeDtypeStruct((steps, tokens, width), jnp.bfloat16)] * parts
        + [jax.ShapeDtypeStruct((tokens // GROUP, rows, width), jnp.float32)],
        name="forward",
    )(kron, thr, *sources)
    return found[:parts], found[parts]


def parts_of(mg):
    high = mg.astype(jnp.bfloat16)
    return high, (mg - high.astype(jnp.float32)).astype(jnp.bfloat16)


def backward_kernel(parts, kron_ref, surrogate_ref, *refs):
    grads, outs = refs[:parts], refs[parts:]
    steps, group, width = grads[0].shape
    rows = steps * group
    kron = kron_ref[...]
    tile = 256
    for at in range(0, width, tile):
        mg = rows_of(grads, at, tile).astype(jnp.float32) * surrogate_ref[0, :, at : at + tile]
        grad = jnp.dot(kron, mg.astype(jnp.bfloat16), preferred_element_type=jnp.float32)
        grad = grad.astype(jnp.bfloat16)
        for k in range(parts):
            outs[k][:, :, at : at + tile] = grad[k * rows : (k + 1) * rows].reshape(
                steps, group, tile
            )


def backward(kron, surrogate, grads):
    parts = len(grads)
    steps, tokens, width = grads[0].shape
    rows = parts * steps * GROUP
    piece = pl.BlockSpec((steps, GROUP, width), lambda g: (0, g, 0))
    return pl.pallas_call(
        functools.partial(backward_kernel, parts),
        grid=(tokens // GROUP,),
        in_specs=[
            pl.BlockSpec(kron.shape, lambda g: (0, 0)),
            pl.BlockSpec((1, rows, width), lambda g: (g, 0, 0)),
        ]
        + [piece] * parts,
        out_specs=[piece] * parts,
        out_shape=[jax.ShapeDtypeStruct((steps, tokens, width), jnp.bfloat16)] * parts,
        cost_estimate=pl.CostEstimate(
            flops=2 * rows * rows * width * (tokens // GROUP),
            bytes_accessed=2 * rows * width * (tokens // GROUP),
            transcendentals=0,
        ),
        name="backward",
    )(kron, surrogate, *grads)


def cross_of(grads, surrogate, sources, cross_ref, tsum_ref, both_ref):
    width = sources[0].shape[-1]
    every = tsum_ref.shape[0]

    @pl.when(pl.program_id(0) == 0)
    def _():
        cross_ref[...] = jnp.zeros_like(cross_ref)
        tsum_ref[...] = jnp.zeros_like(tsum_ref)

    tile = 256
    total = jnp.zeros((every, 128), jnp.float32)
    for at in range(0, width, tile):
        mg = rows_of(grads, at, tile).astype(jnp.float32) * surrogate(at, tile)
        for piece in range(0, tile, 128):
            total = total + mg[:, piece : piece + 128]
        both_ref[:every, at : at + tile], both_ref[every:, at : at + tile] = parts_of(mg)
    tsum_ref[...] += total
    cross = lax.dot_general(
        both_ref[...],
        rows_of(sources, 0, width),
        (((1,), (1,)), ((), ())),
        preferred_element_type=jnp.float32,
    )
    cross_ref[...] += cross[:every] + cross[every:]


def packed(pick, ours, cross, tsum, out_rows):
    total = pick.shape[1]
    one = jnp.where(pick, 1.0, 0.0)
    left = ours(one)
    exact = functools.partial(
        lax.dot_general, precision=lax.Precision.HIGHEST, preferred_element_type=jnp.float32
    )
    low = lambda dim: jnp.bitwise_and(iota2(cross.shape, dim), GROUP - 1)
    narrow = exact(jnp.where(low(0) == low(1), cross, 0.0), one, (((1,), (0,)), ((), ())))
    weights = exact(left, narrow, (((0,), (0,)), ((), ())))
    row_sum = -jnp.sum(tsum, axis=1, keepdims=True)
    thresholds = jnp.broadcast_to(jnp.sum(left * row_sum, axis=0, keepdims=True), (8, total))
    found = jnp.concatenate([weights, thresholds], axis=0)
    found = jnp.concatenate([found, jnp.zeros((total + 8, 128 - total), jnp.float32)], axis=1)
    return jnp.concatenate([found, jnp.zeros((out_rows - total - 8, 128), jnp.float32)], axis=0)


def early_kernel(parts, info_ref, surrogate_ref, bias_ref, *refs):
    sources, grads, rest = refs[:parts], refs[parts : 2 * parts - 1], refs[2 * parts - 1 :]
    out_ref, cross_ref, tsum_ref, both_ref = rest
    steps = sources[0].shape[0]
    rows = steps * GROUP
    others = lambda value: jnp.concatenate([value[: 2 * rows], value[3 * rows :]], axis=0)
    cross_of(
        grads,
        lambda at, tile: others(surrogate_ref[0, :, at : at + tile]),
        sources,
        cross_ref,
        tsum_ref,
        both_ref,
    )

    @pl.when(pl.program_id(0) == pl.num_programs(0) - 1)
    def _():
        pick = selector(info_ref[0], parts, steps)
        out_ref[...] = packed(pick, others, cross_ref[...], tsum_ref[...], out_ref.shape[0])
        first = pick.shape[1] + 8
        out_ref[first : first + bias_ref.shape[0], :] = bias_ref[...]


def late_kernel(parts, info_ref, surrogate_ref, early_ref, *refs):
    sources, (grad_ref, out_ref, cross_ref, tsum_ref, both_ref) = refs[:parts], refs[parts:]
    steps = grad_ref.shape[0]
    rows = steps * GROUP
    cross_of(
        [grad_ref],
        lambda at, tile: surrogate_ref[0, :, at : at + tile],
        sources,
        cross_ref,
        tsum_ref,
        both_ref,
    )

    @pl.when(pl.program_id(0) == pl.num_programs(0) - 1)
    def _():
        pick = selector(info_ref[0], parts, steps)
        out_ref[...] = early_ref[...] + packed(
            pick,
            lambda value: value[2 * rows : 3 * rows],
            cross_ref[...],
            tsum_ref[...],
            out_ref.shape[0],
        )


def small_sums(info, surrogate, extra, sources, grads):
    parts = len(sources)
    steps, share, width = sources[0].shape
    rows = steps * GROUP
    late = len(grads) == 1
    every = len(grads) * rows
    piece = pl.BlockSpec((steps, GROUP, width), lambda g: (0, g, 0))
    fixed = lambda shape: pl.BlockSpec(shape, lambda g: (0, 0))
    out_rows = extra.shape[0] if late else parts * steps + 8 + -(-extra.shape[0] // 8) * 8
    if late:
        some = pl.BlockSpec((1, rows, width), lambda g: (g, 2, 0))
        cost = pl.CostEstimate(
            flops=8 * parts * parts * rows * rows * width * (share // GROUP),
            bytes_accessed=8 * parts * rows * width * (share // GROUP),
            transcendentals=0,
        )
    else:
        some = pl.BlockSpec((1, parts * rows, width), lambda g: (g, 0, 0))
        cost = SMALL
    return pl.pallas_call(
        functools.partial(late_kernel if late else early_kernel, parts),
        grid=(share // GROUP,),
        in_specs=[SMEM, some, fixed(extra.shape)] + [piece] * (parts + len(grads)),
        out_specs=fixed((out_rows, 128)),
        out_shape=jax.ShapeDtypeStruct((out_rows, 128), jnp.float32),
        scratch_shapes=[
            pltpu.VMEM((every, parts * rows), jnp.float32),
            pltpu.VMEM((every, 128), jnp.float32),
            pltpu.VMEM((2 * every, width), jnp.bfloat16),
        ],
        cost_estimate=cost,
        name="late_sums" if late else "early_sums",
    )(info, surrogate, extra, *sources, *grads)


HBM = pl.BlockSpec(memory_space=pl.ANY)


def place_kernel(slots, info_ref, *refs):
    pieces, (whole_ref, held_ref, in_sems, out_sems) = refs[: len(slots)], refs[len(slots) :]
    share = held_ref.shape[2]
    loads, stores = [], []
    for n, slot in enumerate(slots):
        at = pl.multiple_of(info_ref[slot] * share, share)
        loads.append(pltpu.make_async_copy(pieces[n], held_ref.at[n], in_sems.at[n]))
        stores.append(
            pltpu.make_async_copy(
                held_ref.at[n], whole_ref.at[:, pl.ds(at, share), :], out_sems.at[n]
            )
        )
    for load in loads:
        load.start()
    for load, store in zip(loads, stores):
        load.wait()
        store.start()
    for store in stores:
        store.wait()


def place(info, pieces, slots, tokens):
    steps, share, width = pieces[0].shape
    count = len(pieces)
    return pl.pallas_call(
        functools.partial(place_kernel, tuple(slots)),
        in_specs=[SMEM] + [HBM] * count,
        out_specs=HBM,
        out_shape=jax.ShapeDtypeStruct((steps, tokens, width), jnp.bfloat16),
        scratch_shapes=[
            pltpu.VMEM((count, steps, share, width), jnp.bfloat16),
            pltpu.SemaphoreType.DMA((count,)),
            pltpu.SemaphoreType.DMA((count,)),
        ],
        cost_estimate=SMALL,
        name="place",
    )(info, *pieces)


def combine_kernel(shapes, counts, extra, joined, info_ref, *refs):
    halves = len(shapes)
    keeps, refs = refs[:halves], refs[halves:]
    gots = []
    for count in counts:
        gots.append(refs[:count])
        refs = refs[count:]
    adds, outs = refs[:extra], refs[extra:]
    for h, (before, behind, slot) in enumerate(shapes):
        keep_ref = keeps[h]
        stay_ref, send_ref = (outs[0], outs[1]) if joined else (outs[2 * h], outs[2 * h + 1])
        beta = info_ref[slot]
        each = keep_ref.shape[0] // counts[h]
        cols = slice(h * keep_ref.shape[2], (h + 1) * keep_ref.shape[2]) if joined else slice(None)

        def value(p, b, q):
            at = (p * 2 + b) * behind + q
            if counts[h] == 1:
                got = gots[h][0][at]
            else:
                part = (p * 2 * behind) // each
                got = gots[h][part][at - part * each]
            return keep_ref[at] + got.astype(jnp.float32)

        for p in range(before):
            for q in range(behind):
                stay_ref[p * behind + q, :, cols] = value(p, beta, q)
                send_ref[p * behind + q, :, cols] = value(p, 1 - beta, q).astype(send_ref.dtype)
    if extra:
        total = adds[0][...]
        for ref in adds[1:]:
            total = total + ref[...]
        outs[-1][...] = total


def combine(info, shapes, halves, adds=(), joined=False):
    out = []
    for (keep, _), (before, behind, _) in zip(halves[:1] if joined else halves, shapes):
        cols = keep.shape[2] * (len(halves) if joined else 1)
        shape = (before * behind, keep.shape[1], cols)
        out += [
            jax.ShapeDtypeStruct(shape, jnp.float32),
            jax.ShapeDtypeStruct(shape, jnp.bfloat16),
        ]
    if adds:
        out.append(jax.ShapeDtypeStruct(adds[0].shape, jnp.float32))
    args = [k for k, _ in halves] + [g for _, got in halves for g in got] + list(adds)
    counts = tuple(len(got) for _, got in halves)
    found = pl.pallas_call(
        functools.partial(combine_kernel, tuple(shapes), counts, len(adds), joined),
        in_specs=[SMEM] + [VMEM] * len(args),
        out_specs=[VMEM] * len(out),
        out_shape=out,
        cost_estimate=SMALL,
        name="combine",
    )(info, *args)
    pairs = [(found[n], found[n + 1]) for n in range(0, len(out) - len(out) % 2, 2)]
    return pairs, found[-1]


def final_kernel(total, biases, keep_ref, got_ref, *refs):
    sums_refs, (out_ref, mix_ref, thr_ref, bias_ref) = refs[:-4], refs[-4:]
    out_ref[...] = (keep_ref[...] + got_ref[...].astype(jnp.float32)).astype(jnp.bfloat16)
    sums = sums_refs[0][...]
    for ref in sums_refs[1:]:
        sums = sums + ref[...]
    mix_ref[...] = sums[:total, :total]
    thr_ref[...] = sums[total : total + 1, :total]
    bias_ref[...] = sums[total + 8 : total + 8 + biases]


def final(keep, got, sums, total, width):
    shape = jax.ShapeDtypeStruct
    return pl.pallas_call(
        functools.partial(final_kernel, total, width // 128),
        in_specs=[VMEM] * (2 + len(sums)),
        out_specs=[VMEM] * 4,
        out_shape=[
            shape(keep.shape, jnp.bfloat16),
            shape((total, total), jnp.float32),
            shape((1, total), jnp.float32),
            shape((width // 128, 128), jnp.float32),
        ],
        cost_estimate=SMALL,
        name="final",
    )(keep, got, *sums)


def weight_kernel(shard, parts, info_ref, *refs):
    spikes, cots, outs = refs[:parts], refs[parts : 2 * parts], refs[2 * parts : -1]
    part_ref = refs[-1]
    half = part_ref.shape[2]
    core = jnp.bitwise_and(info_ref[0], 1)
    turned = rows_of(spikes, 0, spikes[0].shape[-1]).T
    for side in range(2):
        part_ref[side] = jnp.dot(
            turned, rows_of(cots, side * half, half), preferred_element_type=jnp.float32
        )
    count = part_ref.shape[1] // shard // 2
    step = pl.program_id(0)
    for side in range(2):
        for n in range(count):
            at = lambda odd: pl.ds(pl.multiple_of((2 * n + odd) * shard, 8), shard)
            outs[side][n] = part_ref[side, at(core), :]
            send = part_ref[side, at(1 - core), :].astype(jnp.bfloat16)
            for now in range(2):

                @pl.when(step == now)
                def _():
                    outs[2 + 2 * side + now][n] = send


def weight_halves(info, spikes, cots, shard):
    steps, tokens, width = spikes[0].shape
    block, cols = width // 2, width // 2
    count = block // shard // 2
    send = jax.ShapeDtypeStruct((count, shard, cols), jnp.bfloat16)
    keep = jax.ShapeDtypeStruct((2 * count, shard, cols), jnp.float32)
    found = pl.pallas_call(
        functools.partial(weight_kernel, shard, len(spikes)),
        grid=(2,),
        in_specs=[SMEM]
        + [pl.BlockSpec((steps, tokens, block), lambda i: (0, 0, i))] * len(spikes)
        + [pl.BlockSpec((steps, tokens, width), lambda i: (0, 0, 0))] * len(spikes),
        out_specs=[pl.BlockSpec((count, shard, cols), lambda i: (i, 0, 0))] * 2
        + [pl.BlockSpec((count, shard, cols), lambda i: (0, 0, 0))] * 4,
        out_shape=[keep, keep] + [send] * 4,
        scratch_shapes=[pltpu.VMEM((2, block, cols), jnp.float32)],
        cost_estimate=SMALL,
        name="weight_halves",
    )(info, *spikes, *cots)
    return [(found[0], found[2:4]), (found[1], found[4:6])]


def body(ndp, ntm, currents, mixing, threshold, weight, bias, cotangent):
    _, steps, tokens, width = currents.shape
    me = lax.axis_index("tm")
    bits = lambda n: n.bit_length() - 1
    share = tokens // ntm
    bdp, btm = bits(ndp), bits(ntm)
    names = [("dp", b) for b in range(bdp - 1, -1, -1)] + [("tm", b) for b in range(btm - 1, -1, -1)]
    sizes = {"dp": ndp, "tm": ntm}
    info = jnp.stack(
        [me]
        + [(lax.axis_index(axis) >> b) & 1 for axis, b in names]
        + [me ^ k for k in range(ntm)]
    )
    slot = lambda bit: 1 + names.index(bit)
    spot = lambda k: 1 + len(names) + k

    def exchange(pieces):
        return [pieces[0]] + [xor_permute(pieces[k], "tm", ntm, k) for k in range(1, ntm)]

    def cut(value):
        found = {}
        for k in list(range(2, ntm)) + [1, 0]:
            found[k] = lax.dynamic_slice_in_dim(value, (me ^ k) * share, share, axis=1)
            value = after(value, found[k])
        return [found[k] for k in range(ntm)]

    flat = lambda value: value.reshape(-1, width)
    pieces = cut(currents[0])
    currents_in = exchange(pieces)
    cots = exchange(cut(after(cotangent[0], *pieces[1:])))
    kron_fwd, kron_bwd, thr_rows = build_krons(info, mixing, threshold, ntm, steps)

    def spike_grad(cot):
        grad = jnp.einsum("re,de->rd", flat(cot), weight, preferred_element_type=jnp.float32)
        return grad.astype(jnp.bfloat16).reshape(cot.shape)

    bias_term = jnp.sum(flat(cotangent).astype(jnp.float32), axis=0)
    grads = [spike_grad(cot) for cot in cots[:2]]
    spikes, surrogate = forward(kron_fwd, after(thr_rows, bias_term, *grads), currents_in)
    outs = [
        (jnp.dot(flat(spikes[k]), weight, preferred_element_type=jnp.float32) + bias)
        .astype(jnp.bfloat16)
        .reshape(steps, share, width)
        for k in range(ntm)
    ]
    outs_in = exchange(outs)
    grads.append(None)
    grads += [spike_grad(after(cot, *outs)) for cot in cots[3:]]

    others = [k for k in range(ntm) if k != 2]
    early = small_sums(
        info,
        after(surrogate, *outs),
        bias_term.reshape(-1, 128),
        currents_in,
        [grads[k] for k in others],
    )

    shard = width // (ndp * ntm)
    core, y = ("tm", 0), ("dp", 0)
    zs, xs = [("dp", b) for b in range(1, bdp)], [("tm", b) for b in range(1, btm)]
    half = width // 2
    left = names[:-1]

    if shard % 8 == 0:
        late = cots[:2] + [after(cots[2], *outs, early)] + cots[3:]
        halves = weight_halves(info, spikes, late, shard)
    else:
        whole = sum(
            jnp.einsum("rd,re->de", flat(a), flat(b), preferred_element_type=jnp.float32)
            for a, b in zip(spikes, cots)
        ).reshape(-1, 2, shard, width)
        pick = lambda b: lax.dynamic_index_in_dim(whole, b, 1, keepdims=False)
        keep, send = pick(me & 1), pick(1 - (me & 1)).astype(jnp.bfloat16)
        halves = [(keep[..., c : c + half], [send[..., c : c + half]]) for c in (0, half)]

    sent = halves[-1][1][0]
    routes = ([y] + zs[:1], zs[:1] + [y])

    def go(value, *path):
        if all(axis == path[0][0] for axis, _ in path):
            axis = path[0][0]
            return xor_permute(value, axis, sizes[axis], sum(1 << b for _, b in path))
        mask = sum((1 << b) * (ntm if axis == "dp" else 1) for axis, b in path)
        return xor_permute(value, ("dp", "tm"), ndp * ntm, mask)

    def step(state, lefts, bits, joined=False):
        shapes = []
        for rest, bit in zip(lefts, bits):
            p = rest.index(bit)
            shapes.append((1 << p, 1 << (len(rest) - p - 1), slot(bit)))
        pairs, _ = combine(info, shapes, state, (), joined)
        return pairs, [[x for x in rest if x != bit] for rest, bit in zip(lefts, bits)]

    def travel(pairs, bits):
        return [(keep, [go(send, bit)]) for (keep, send), bit in zip(pairs, bits)]

    state = [(keep, [go(after(send, sent), core) for send in sends]) for keep, sends in halves]
    bits = [route[0] for route in routes]
    pairs, lefts = step(state, [left, left], bits)
    state = travel(pairs, bits)
    grads[2] = spike_grad(after(cots[2], outs_in[-1], *[send for _, send in pairs]))
    cgrads = list(backward(kron_bwd, surrogate, grads))
    cgrads_in = exchange(cgrads)

    def meet(sums, *bits):
        for bit in bits:
            sums = sums + go(sums, bit)
        return sums

    spots = list(map(spot, range(ntm)))

    def gated(state, *gate):
        return [(after(state[0][0], *gate), state[0][1])] + state[1:]

    bits = [route[1] for route in routes]
    pairs, lefts = step(gated(state, *outs_in[1:3], *cgrads), lefts, bits)
    state = travel(pairs, bits)
    sends = [send for _, send in pairs]
    sums = small_sums(info, after(surrogate, *sends), early, currents_in, grads[2:3])
    hops, gate = [core, y] + zs, [sums, cgrads_in[1]]
    for bit in zs[1:]:
        pairs, lefts = step(gated(state, *gate), lefts, [bit] * len(state), joined=len(state) > 1)
        lefts = lefts[:1]
        state = travel(pairs, [bit])
        sums = after(sums, pairs[0][1])
        if bit == zs[1]:
            sums = meet(sums, core)
            output = place(info, [after(outs_in[0], sums)] + outs_in[1:], spots, tokens)
            sums = meet(after(sums, output) + go(sums, y), hops[2])
            hops = hops[3:]
        else:
            sums, hops = meet(sums, hops[0]), hops[1:]
        gate = [sums]

    pairs, lefts = step(gated(state, *gate), lefts, xs[:1])
    keep, send = pairs[0]
    got = go(send, xs[0])
    current_grad = place(info, [after(cgrads_in[0], send)] + cgrads_in[1:], spots, tokens)
    rest = lefts[0]
    for bit in xs[1:]:
        pairs, (rest,) = step([(keep, [got])], [rest], [bit])
        keep, send = pairs[0]
        got = go(send, bit)
    hops += xs
    sums = after(sums, send)
    sums = [sums] + [
        go(sums, *[bit for i, bit in enumerate(hops) if n >> i & 1])
        for n in range(1, 1 << len(hops))
    ]
    weight_grad, mixing_grad, threshold_grad, bias_grad = final(
        keep.reshape(shard, width), got.reshape(shard, width), sums, ntm * steps, width
    )
    return (
        output[None],
        current_grad[None],
        weight_grad,
        mixing_grad,
        threshold_grad.reshape(-1),
        bias_grad.reshape(-1),
    )


def solution(mesh):
    return jax.shard_map(
        functools.partial(body, mesh.shape["dp"], mesh.shape["tm"]),
        mesh=mesh,
        in_specs=(P("dp", "tm", None, None), P(), P(), P(), P(), P("dp", "tm", None, None)),
        out_specs=(
            P("dp", "tm", None, None),
            P("dp", "tm", None, None),
            P(("dp", "tm"), None),
            P(),
            P(),
            P(),
        ),
        check_vma=False,
    )
```

```python
import functools

import jax
import jax.numpy as jnp
from jax import lax
from jax.experimental import pallas as pl
from jax.experimental.pallas import tpu as pltpu
from jax.sharding import PartitionSpec as P

GROUP = 16
SMALL = pl.CostEstimate(flops=1000, bytes_accessed=1000, transcendentals=0)
SMEM = pl.BlockSpec(memory_space=pltpu.SMEM)
VMEM = pl.BlockSpec(memory_space=pltpu.VMEM)


def xor_permute(value, axis, size, mask):
    return lax.ppermute(value, axis, [(i, i ^ mask) for i in range(size)])


def after(value, *earlier):
    return lax.optimization_barrier((value, *earlier))[0]


def iota2(shape, dim):
    return lax.broadcasted_iota(jnp.int32, shape, dim)


def selector(me, parts, steps):
    rows, total = parts * steps * GROUP, parts * steps
    depth, shift = (steps * GROUP).bit_length() - 1, GROUP.bit_length() - 1
    at = iota2((rows, total), 0)
    source = jnp.bitwise_xor(me, lax.shift_right_logical(at, depth))
    step = jnp.bitwise_and(lax.shift_right_logical(at, shift), steps - 1)
    return source * steps + step == iota2((rows, total), 1)


def same_token(rows):
    low = lambda dim: jnp.bitwise_and(iota2((rows, rows), dim), GROUP - 1)
    return low(0) == low(1)


def kron_kernel(parts, steps, me_ref, mixing_ref, thr_ref, fwd_ref, bwd_ref, rows_ref):
    pick = selector(me_ref[0], parts, steps)
    one = jnp.where(pick, 1.0, 0.0).astype(jnp.bfloat16)
    mixing = mixing_ref[...].astype(jnp.bfloat16)
    same = same_token(pick.shape[0])
    dot = functools.partial(lax.dot_general, preferred_element_type=jnp.float32)
    for ref, dim in ((fwd_ref, 0), (bwd_ref, 1)):
        first = dot(one, mixing, (((1,), (dim,)), ((), ()))).astype(jnp.bfloat16)
        wide = dot(first, one, (((1,), (1,)), ((), ())))
        ref[...] = jnp.where(same, wide, 0.0).astype(jnp.bfloat16)
    thr = jnp.broadcast_to(thr_ref[...], pick.shape)
    rows_ref[...] = jnp.sum(jnp.where(pick, thr, 0.0), axis=1, keepdims=True)


def build_krons(info, mixing, threshold, parts, steps):
    rows = parts * steps * GROUP
    vmem = pl.BlockSpec(memory_space=pltpu.VMEM)
    wide = jax.ShapeDtypeStruct((rows, rows), jnp.bfloat16)
    return pl.pallas_call(
        functools.partial(kron_kernel, parts, steps),
        in_specs=[pl.BlockSpec(memory_space=pltpu.SMEM), vmem, vmem],
        out_specs=(vmem, vmem, vmem),
        out_shape=(wide, wide, jax.ShapeDtypeStruct((rows, 1), jnp.float32)),
        name="build_krons",
    )(info, mixing, threshold.reshape(1, -1))


def rows_of(refs, at, tile):
    return jnp.concatenate([r[:, :, at : at + tile].reshape(-1, tile) for r in refs], axis=0)


def forward_kernel(parts, kron_ref, thr_ref, *refs):
    sources, spikes, surrogate_ref = refs[:parts], refs[parts : 2 * parts], refs[-1]
    steps, group, width = sources[0].shape
    rows = steps * group
    kron = kron_ref[...]
    thr = thr_ref[...]
    tile = 256
    for at in range(0, width, tile):
        cur = rows_of(sources, at, tile)
        shifted = jnp.dot(kron, cur, preferred_element_type=jnp.float32) - thr
        fired = jnp.where(shifted > 0, 1.0, 0.0).astype(jnp.bfloat16)
        for k in range(parts):
            spikes[k][:, :, at : at + tile] = fired[k * rows : (k + 1) * rows].reshape(
                steps, group, tile
            )
        small = jnp.exp(-jnp.abs(shifted))
        part = 1.0 / (1.0 + small)
        surrogate_ref[0, :, at : at + tile] = small * part * part


def forward(kron, thr, sources):
    parts = len(sources)
    steps, tokens, width = sources[0].shape
    piece = pl.BlockSpec((steps, GROUP, width), lambda g: (0, g, 0))
    fixed = lambda shape: pl.BlockSpec(shape, lambda g: (0, 0))
    rows = parts * steps * GROUP
    found = pl.pallas_call(
        functools.partial(forward_kernel, parts),
        grid=(tokens // GROUP,),
        in_specs=[fixed(kron.shape), fixed(thr.shape)] + [piece] * parts,
        out_specs=[piece] * parts + [pl.BlockSpec((1, rows, width), lambda g: (g, 0, 0))],
        out_shape=[jax.ShapeDtypeStruct((steps, tokens, width), jnp.bfloat16)] * parts
        + [jax.ShapeDtypeStruct((tokens // GROUP, rows, width), jnp.float32)],
        name="forward",
    )(kron, thr, *sources)
    return found[:parts], found[parts]


def parts_of(mg):
    high = mg.astype(jnp.bfloat16)
    return high, (mg - high.astype(jnp.float32)).astype(jnp.bfloat16)


def backward_kernel(parts, kron_ref, surrogate_ref, *refs):
    grads, outs = refs[:parts], refs[parts:]
    steps, group, width = grads[0].shape
    rows = steps * group
    kron = kron_ref[...]
    tile = 256
    for at in range(0, width, tile):
        mg = rows_of(grads, at, tile).astype(jnp.float32) * surrogate_ref[0, :, at : at + tile]
        grad = jnp.dot(kron, mg.astype(jnp.bfloat16), preferred_element_type=jnp.float32)
        grad = grad.astype(jnp.bfloat16)
        for k in range(parts):
            outs[k][:, :, at : at + tile] = grad[k * rows : (k + 1) * rows].reshape(
                steps, group, tile
            )


def backward(kron, surrogate, grads):
    parts = len(grads)
    steps, tokens, width = grads[0].shape
    rows = parts * steps * GROUP
    piece = pl.BlockSpec((steps, GROUP, width), lambda g: (0, g, 0))
    return pl.pallas_call(
        functools.partial(backward_kernel, parts),
        grid=(tokens // GROUP,),
        in_specs=[
            pl.BlockSpec(kron.shape, lambda g: (0, 0)),
            pl.BlockSpec((1, rows, width), lambda g: (g, 0, 0)),
        ]
        + [piece] * parts,
        out_specs=[piece] * parts,
        out_shape=[jax.ShapeDtypeStruct((steps, tokens, width), jnp.bfloat16)] * parts,
        cost_estimate=pl.CostEstimate(
            flops=2 * rows * rows * width * (tokens // GROUP),
            bytes_accessed=2 * rows * width * (tokens // GROUP),
            transcendentals=0,
        ),
        name="backward",
    )(kron, surrogate, *grads)


def cross_of(grads, surrogate, sources, cross_ref, tsum_ref, both_ref):
    width = sources[0].shape[-1]
    every = tsum_ref.shape[0]

    @pl.when(pl.program_id(0) == 0)
    def _():
        cross_ref[...] = jnp.zeros_like(cross_ref)
        tsum_ref[...] = jnp.zeros_like(tsum_ref)

    tile = 256
    total = jnp.zeros((every, 128), jnp.float32)
    for at in range(0, width, tile):
        mg = rows_of(grads, at, tile).astype(jnp.float32) * surrogate(at, tile)
        for piece in range(0, tile, 128):
            total = total + mg[:, piece : piece + 128]
        both_ref[:every, at : at + tile], both_ref[every:, at : at + tile] = parts_of(mg)
    tsum_ref[...] += total
    cross = lax.dot_general(
        both_ref[...],
        rows_of(sources, 0, width),
        (((1,), (1,)), ((), ())),
        preferred_element_type=jnp.float32,
    )
    cross_ref[...] += cross[:every] + cross[every:]


def packed(pick, ours, cross, tsum, out_rows):
    total = pick.shape[1]
    one = jnp.where(pick, 1.0, 0.0)
    left = ours(one)
    exact = functools.partial(
        lax.dot_general, precision=lax.Precision.HIGHEST, preferred_element_type=jnp.float32
    )
    low = lambda dim: jnp.bitwise_and(iota2(cross.shape, dim), GROUP - 1)
    narrow = exact(jnp.where(low(0) == low(1), cross, 0.0), one, (((1,), (0,)), ((), ())))
    weights = exact(left, narrow, (((0,), (0,)), ((), ())))
    row_sum = -jnp.sum(tsum, axis=1, keepdims=True)
    thresholds = jnp.broadcast_to(jnp.sum(left * row_sum, axis=0, keepdims=True), (8, total))
    found = jnp.concatenate([weights, thresholds], axis=0)
    found = jnp.concatenate([found, jnp.zeros((total + 8, 128 - total), jnp.float32)], axis=1)
    return jnp.concatenate([found, jnp.zeros((out_rows - total - 8, 128), jnp.float32)], axis=0)


def early_kernel(parts, info_ref, surrogate_ref, bias_ref, *refs):
    sources, grads, rest = refs[:parts], refs[parts : 2 * parts - 1], refs[2 * parts - 1 :]
    out_ref, cross_ref, tsum_ref, both_ref = rest
    steps = sources[0].shape[0]
    rows = steps * GROUP
    others = lambda value: jnp.concatenate([value[: 2 * rows], value[3 * rows :]], axis=0)
    cross_of(
        grads,
        lambda at, tile: others(surrogate_ref[0, :, at : at + tile]),
        sources,
        cross_ref,
        tsum_ref,
        both_ref,
    )

    @pl.when(pl.program_id(0) == pl.num_programs(0) - 1)
    def _():
        pick = selector(info_ref[0], parts, steps)
        out_ref[...] = packed(pick, others, cross_ref[...], tsum_ref[...], out_ref.shape[0])
        first = pick.shape[1] + 8
        out_ref[first : first + bias_ref.shape[0], :] = bias_ref[...]


def late_kernel(parts, info_ref, surrogate_ref, early_ref, *refs):
    sources, (grad_ref, out_ref, cross_ref, tsum_ref, both_ref) = refs[:parts], refs[parts:]
    steps = grad_ref.shape[0]
    rows = steps * GROUP
    cross_of(
        [grad_ref],
        lambda at, tile: surrogate_ref[0, :, at : at + tile],
        sources,
        cross_ref,
        tsum_ref,
        both_ref,
    )

    @pl.when(pl.program_id(0) == pl.num_programs(0) - 1)
    def _():
        pick = selector(info_ref[0], parts, steps)
        out_ref[...] = early_ref[...] + packed(
            pick,
            lambda value: value[2 * rows : 3 * rows],
            cross_ref[...],
            tsum_ref[...],
            out_ref.shape[0],
        )


def small_sums(info, surrogate, extra, sources, grads):
    parts = len(sources)
    steps, share, width = sources[0].shape
    rows = steps * GROUP
    late = len(grads) == 1
    every = len(grads) * rows
    piece = pl.BlockSpec((steps, GROUP, width), lambda g: (0, g, 0))
    fixed = lambda shape: pl.BlockSpec(shape, lambda g: (0, 0))
    out_rows = extra.shape[0] if late else parts * steps + 8 + -(-extra.shape[0] // 8) * 8
    if late:
        some = pl.BlockSpec((1, rows, width), lambda g: (g, 2, 0))
        cost = pl.CostEstimate(
            flops=8 * parts * parts * rows * rows * width * (share // GROUP),
            bytes_accessed=8 * parts * rows * width * (share // GROUP),
            transcendentals=0,
        )
    else:
        some = pl.BlockSpec((1, parts * rows, width), lambda g: (g, 0, 0))
        cost = SMALL
    return pl.pallas_call(
        functools.partial(late_kernel if late else early_kernel, parts),
        grid=(share // GROUP,),
        in_specs=[SMEM, some, fixed(extra.shape)] + [piece] * (parts + len(grads)),
        out_specs=fixed((out_rows, 128)),
        out_shape=jax.ShapeDtypeStruct((out_rows, 128), jnp.float32),
        scratch_shapes=[
            pltpu.VMEM((every, parts * rows), jnp.float32),
            pltpu.VMEM((every, 128), jnp.float32),
            pltpu.VMEM((2 * every, width), jnp.bfloat16),
        ],
        cost_estimate=cost,
        name="late_sums" if late else "early_sums",
    )(info, surrogate, extra, *sources, *grads)


HBM = pl.BlockSpec(memory_space=pl.ANY)


def place_kernel(slots, info_ref, *refs):
    pieces, (whole_ref, held_ref, in_sems, out_sems) = refs[: len(slots)], refs[len(slots) :]
    share = held_ref.shape[2]
    loads, stores = [], []
    for n, slot in enumerate(slots):
        at = pl.multiple_of(info_ref[slot] * share, share)
        loads.append(pltpu.make_async_copy(pieces[n], held_ref.at[n], in_sems.at[n]))
        stores.append(
            pltpu.make_async_copy(
                held_ref.at[n], whole_ref.at[:, pl.ds(at, share), :], out_sems.at[n]
            )
        )
    for load in loads:
        load.start()
    for load, store in zip(loads, stores):
        load.wait()
        store.start()
    for store in stores:
        store.wait()


def place(info, pieces, slots, tokens):
    steps, share, width = pieces[0].shape
    count = len(pieces)
    return pl.pallas_call(
        functools.partial(place_kernel, tuple(slots)),
        in_specs=[SMEM] + [HBM] * count,
        out_specs=HBM,
        out_shape=jax.ShapeDtypeStruct((steps, tokens, width), jnp.bfloat16),
        scratch_shapes=[
            pltpu.VMEM((count, steps, share, width), jnp.bfloat16),
            pltpu.SemaphoreType.DMA((count,)),
            pltpu.SemaphoreType.DMA((count,)),
        ],
        cost_estimate=SMALL,
        name="place",
    )(info, *pieces)


def combine_kernel(shapes, counts, extra, joined, info_ref, *refs):
    halves = len(shapes)
    keeps, refs = refs[:halves], refs[halves:]
    gots = []
    for count in counts:
        gots.append(refs[:count])
        refs = refs[count:]
    adds, outs = refs[:extra], refs[extra:]
    for h, (before, behind, slot) in enumerate(shapes):
        keep_ref = keeps[h]
        stay_ref, send_ref = (outs[0], outs[1]) if joined else (outs[2 * h], outs[2 * h + 1])
        beta = info_ref[slot]
        each = keep_ref.shape[0] // counts[h]
        cols = slice(h * keep_ref.shape[2], (h + 1) * keep_ref.shape[2]) if joined else slice(None)

        def value(p, b, q):
            at = (p * 2 + b) * behind + q
            if counts[h] == 1:
                got = gots[h][0][at]
            else:
                part = (p * 2 * behind) // each
                got = gots[h][part][at - part * each]
            return keep_ref[at] + got.astype(jnp.float32)

        for p in range(before):
            for q in range(behind):
                stay_ref[p * behind + q, :, cols] = value(p, beta, q)
                send_ref[p * behind + q, :, cols] = value(p, 1 - beta, q).astype(send_ref.dtype)
    if extra:
        total = adds[0][...]
        for ref in adds[1:]:
            total = total + ref[...]
        outs[-1][...] = total


def combine(info, shapes, halves, adds=(), joined=False):
    out = []
    for (keep, _), (before, behind, _) in zip(halves[:1] if joined else halves, shapes):
        cols = keep.shape[2] * (len(halves) if joined else 1)
        shape = (before * behind, keep.shape[1], cols)
        out += [
            jax.ShapeDtypeStruct(shape, jnp.float32),
            jax.ShapeDtypeStruct(shape, jnp.bfloat16),
        ]
    if adds:
        out.append(jax.ShapeDtypeStruct(adds[0].shape, jnp.float32))
    args = [k for k, _ in halves] + [g for _, got in halves for g in got] + list(adds)
    counts = tuple(len(got) for _, got in halves)
    found = pl.pallas_call(
        functools.partial(combine_kernel, tuple(shapes), counts, len(adds), joined),
        in_specs=[SMEM] + [VMEM] * len(args),
        out_specs=[VMEM] * len(out),
        out_shape=out,
        cost_estimate=SMALL,
        name="combine",
    )(info, *args)
    pairs = [(found[n], found[n + 1]) for n in range(0, len(out) - len(out) % 2, 2)]
    return pairs, found[-1]


def final_kernel(total, biases, keep_ref, got_ref, *refs):
    sums_refs, (out_ref, mix_ref, thr_ref, bias_ref) = refs[:-4], refs[-4:]
    out_ref[...] = (keep_ref[...] + got_ref[...].astype(jnp.float32)).astype(jnp.bfloat16)
    sums = sums_refs[0][...]
    for ref in sums_refs[1:]:
        sums = sums + ref[...]
    mix_ref[...] = sums[:total, :total]
    thr_ref[...] = sums[total : total + 1, :total]
    bias_ref[...] = sums[total + 8 : total + 8 + biases]


def final(keep, got, sums, total, width):
    shape = jax.ShapeDtypeStruct
    return pl.pallas_call(
        functools.partial(final_kernel, total, width // 128),
        in_specs=[VMEM] * (2 + len(sums)),
        out_specs=[VMEM] * 4,
        out_shape=[
            shape(keep.shape, jnp.bfloat16),
            shape((total, total), jnp.float32),
            shape((1, total), jnp.float32),
            shape((width // 128, 128), jnp.float32),
        ],
        cost_estimate=SMALL,
        name="final",
    )(keep, got, *sums)


def weight_kernel(shard, parts, info_ref, *refs):
    spikes, cots, outs = refs[:parts], refs[parts : 2 * parts], refs[2 * parts : -1]
    part_ref = refs[-1]
    half = part_ref.shape[1] // 2
    core = jnp.bitwise_and(info_ref[0], 1)
    part_ref[...] = lax.dot_general(
        rows_of(spikes, 0, spikes[0].shape[-1]),
        rows_of(cots, 0, cots[0].shape[-1]),
        (((0,), (0,)), ((), ())),
        preferred_element_type=jnp.float32,
    )
    count = part_ref.shape[0] // shard // 2
    step = pl.program_id(0)
    for side in range(2):
        for n in range(count):
            at = lambda odd: pl.ds(pl.multiple_of((2 * n + odd) * shard, 8), shard)
            cols = slice(side * half, (side + 1) * half)
            outs[side][n] = part_ref[at(core), cols]
            send = part_ref[at(1 - core), cols].astype(jnp.bfloat16)
            for now in range(2):

                @pl.when(step == now)
                def _():
                    outs[2 + 2 * side + now][n] = send


def weight_halves(info, spikes, cots, shard):
    steps, tokens, width = spikes[0].shape
    block, cols = width // 2, width // 2
    count = block // shard // 2
    send = jax.ShapeDtypeStruct((count, shard, cols), jnp.bfloat16)
    keep = jax.ShapeDtypeStruct((2 * count, shard, cols), jnp.float32)
    found = pl.pallas_call(
        functools.partial(weight_kernel, shard, len(spikes)),
        grid=(2,),
        in_specs=[SMEM]
        + [pl.BlockSpec((steps, tokens, block), lambda i: (0, 0, i))] * len(spikes)
        + [pl.BlockSpec((steps, tokens, width), lambda i: (0, 0, 0))] * len(spikes),
        out_specs=[pl.BlockSpec((count, shard, cols), lambda i: (i, 0, 0))] * 2
        + [pl.BlockSpec((count, shard, cols), lambda i: (0, 0, 0))] * 4,
        out_shape=[keep, keep] + [send] * 4,
        scratch_shapes=[pltpu.VMEM((block, width), jnp.float32)],
        cost_estimate=SMALL,
        name="weight_halves",
    )(info, *spikes, *cots)
    return [(found[0], found[2:4]), (found[1], found[4:6])]


def body(ndp, ntm, currents, mixing, threshold, weight, bias, cotangent):
    _, steps, tokens, width = currents.shape
    me = lax.axis_index("tm")
    bits = lambda n: n.bit_length() - 1
    share = tokens // ntm
    bdp, btm = bits(ndp), bits(ntm)
    names = [("dp", b) for b in range(bdp - 1, -1, -1)] + [("tm", b) for b in range(btm - 1, -1, -1)]
    sizes = {"dp": ndp, "tm": ntm}
    info = jnp.stack(
        [me]
        + [(lax.axis_index(axis) >> b) & 1 for axis, b in names]
        + [me ^ k for k in range(ntm)]
    )
    slot = lambda bit: 1 + names.index(bit)
    spot = lambda k: 1 + len(names) + k

    def exchange(pieces):
        return [pieces[0]] + [xor_permute(pieces[k], "tm", ntm, k) for k in range(1, ntm)]

    def cut(value):
        found = {}
        for k in list(range(2, ntm)) + [1, 0]:
            found[k] = lax.dynamic_slice_in_dim(value, (me ^ k) * share, share, axis=1)
            value = after(value, found[k])
        return [found[k] for k in range(ntm)]

    flat = lambda value: value.reshape(-1, width)
    pieces = cut(currents[0])
    currents_in = exchange(pieces)
    cots = exchange(cut(after(cotangent[0], *pieces[1:])))
    kron_fwd, kron_bwd, thr_rows = build_krons(info, mixing, threshold, ntm, steps)

    def spike_grad(cot):
        grad = jnp.einsum("re,de->rd", flat(cot), weight, preferred_element_type=jnp.float32)
        return grad.astype(jnp.bfloat16).reshape(cot.shape)

    bias_term = jnp.sum(flat(cotangent).astype(jnp.float32), axis=0)
    grads = [spike_grad(cot) for cot in cots[:2]]
    spikes, surrogate = forward(kron_fwd, after(thr_rows, bias_term, *grads), currents_in)
    outs = [
        (jnp.dot(flat(spikes[k]), weight, preferred_element_type=jnp.float32) + bias)
        .astype(jnp.bfloat16)
        .reshape(steps, share, width)
        for k in range(ntm)
    ]
    outs_in = exchange(outs)
    grads.append(None)
    grads += [spike_grad(after(cot, *outs)) for cot in cots[3:]]

    others = [k for k in range(ntm) if k != 2]
    early = small_sums(
        info,
        after(surrogate, *outs),
        bias_term.reshape(-1, 128),
        currents_in,
        [grads[k] for k in others],
    )

    shard = width // (ndp * ntm)
    core, y = ("tm", 0), ("dp", 0)
    zs, xs = [("dp", b) for b in range(1, bdp)], [("tm", b) for b in range(1, btm)]
    half = width // 2
    left = names[:-1]

    if shard % 8 == 0:
        late = cots[:2] + [after(cots[2], *outs, early)] + cots[3:]
        halves = weight_halves(info, spikes, late, shard)
    else:
        whole = sum(
            jnp.einsum("rd,re->de", flat(a), flat(b), preferred_element_type=jnp.float32)
            for a, b in zip(spikes, cots)
        ).reshape(-1, 2, shard, width)
        pick = lambda b: lax.dynamic_index_in_dim(whole, b, 1, keepdims=False)
        keep, send = pick(me & 1), pick(1 - (me & 1)).astype(jnp.bfloat16)
        halves = [(keep[..., c : c + half], [send[..., c : c + half]]) for c in (0, half)]

    sent = halves[-1][1][0]
    routes = ([y] + zs[:1], zs[:1] + [y])

    def go(value, *path):
        if all(axis == path[0][0] for axis, _ in path):
            axis = path[0][0]
            return xor_permute(value, axis, sizes[axis], sum(1 << b for _, b in path))
        mask = sum((1 << b) * (ntm if axis == "dp" else 1) for axis, b in path)
        return xor_permute(value, ("dp", "tm"), ndp * ntm, mask)

    def step(state, lefts, bits, joined=False):
        shapes = []
        for rest, bit in zip(lefts, bits):
            p = rest.index(bit)
            shapes.append((1 << p, 1 << (len(rest) - p - 1), slot(bit)))
        pairs, _ = combine(info, shapes, state, (), joined)
        return pairs, [[x for x in rest if x != bit] for rest, bit in zip(lefts, bits)]

    def travel(pairs, bits):
        return [(keep, [go(send, bit)]) for (keep, send), bit in zip(pairs, bits)]

    state = [(keep, [go(after(send, sent), core) for send in sends]) for keep, sends in halves]
    bits = [route[0] for route in routes]
    pairs, lefts = step(state, [left, left], bits)
    state = travel(pairs, bits)
    grads[2] = spike_grad(after(cots[2], outs_in[-1], *[send for _, send in pairs]))
    cgrads = list(backward(kron_bwd, surrogate, grads))
    cgrads_in = exchange(cgrads)

    def meet(sums, *bits):
        for bit in bits:
            sums = sums + go(sums, bit)
        return sums

    spots = list(map(spot, range(ntm)))

    def gated(state, *gate):
        return [(after(state[0][0], *gate), state[0][1])] + state[1:]

    bits = [route[1] for route in routes]
    pairs, lefts = step(gated(state, *outs_in[1:3], *cgrads), lefts, bits)
    state = travel(pairs, bits)
    sends = [send for _, send in pairs]
    sums = small_sums(info, after(surrogate, *sends), early, currents_in, grads[2:3])
    hops, gate = [core, y] + zs, [sums, cgrads_in[1]]
    for bit in zs[1:]:
        pairs, lefts = step(gated(state, *gate), lefts, [bit] * len(state), joined=len(state) > 1)
        lefts = lefts[:1]
        state = travel(pairs, [bit])
        sums = after(sums, pairs[0][1])
        if bit == zs[1]:
            sums = meet(sums, core)
            output = place(info, [after(outs_in[0], sums)] + outs_in[1:], spots, tokens)
            sums = meet(after(sums, output) + go(sums, y), hops[2])
            hops = hops[3:]
        else:
            sums, hops = meet(sums, hops[0]), hops[1:]
        gate = [sums]

    pairs, lefts = step(gated(state, *gate), lefts, xs[:1])
    keep, send = pairs[0]
    got = go(send, xs[0])
    current_grad = place(info, [after(cgrads_in[0], send)] + cgrads_in[1:], spots, tokens)
    rest = lefts[0]
    for bit in xs[1:]:
        pairs, (rest,) = step([(keep, [got])], [rest], [bit])
        keep, send = pairs[0]
        got = go(send, bit)
    hops += xs
    sums = after(sums, send)
    sums = [sums] + [
        go(sums, *[bit for i, bit in enumerate(hops) if n >> i & 1])
        for n in range(1, 1 << len(hops))
    ]
    weight_grad, mixing_grad, threshold_grad, bias_grad = final(
        keep.reshape(shard, width), got.reshape(shard, width), sums, ntm * steps, width
    )
    return (
        output[None],
        current_grad[None],
        weight_grad,
        mixing_grad,
        threshold_grad.reshape(-1),
        bias_grad.reshape(-1),
    )


def solution(mesh):
    return jax.shard_map(
        functools.partial(body, mesh.shape["dp"], mesh.shape["tm"]),
        mesh=mesh,
        in_specs=(P("dp", "tm", None, None), P(), P(), P(), P(), P("dp", "tm", None, None)),
        out_specs=(
            P("dp", "tm", None, None),
            P("dp", "tm", None, None),
            P(("dp", "tm"), None),
            P(),
            P(),
            P(),
        ),
        check_vma=False,
    )
```

```python
import functools

import jax
import jax.numpy as jnp
from jax import lax
from jax.experimental import pallas as pl
from jax.experimental.pallas import tpu as pltpu
from jax.sharding import PartitionSpec as P

GROUP = 16
SMALL = pl.CostEstimate(flops=1000, bytes_accessed=1000, transcendentals=0)
SMEM = pl.BlockSpec(memory_space=pltpu.SMEM)
VMEM = pl.BlockSpec(memory_space=pltpu.VMEM)


def xor_permute(value, axis, size, mask):
    return lax.ppermute(value, axis, [(i, i ^ mask) for i in range(size)])


def after(value, *earlier):
    return lax.optimization_barrier((value, *earlier))[0]


def iota2(shape, dim):
    return lax.broadcasted_iota(jnp.int32, shape, dim)


def selector(me, parts, steps):
    rows, total = parts * steps * GROUP, parts * steps
    depth, shift = (steps * GROUP).bit_length() - 1, GROUP.bit_length() - 1
    at = iota2((rows, total), 0)
    source = jnp.bitwise_xor(me, lax.shift_right_logical(at, depth))
    step = jnp.bitwise_and(lax.shift_right_logical(at, shift), steps - 1)
    return source * steps + step == iota2((rows, total), 1)


def same_token(rows):
    low = lambda dim: jnp.bitwise_and(iota2((rows, rows), dim), GROUP - 1)
    return low(0) == low(1)


def kron_kernel(parts, steps, me_ref, mixing_ref, thr_ref, fwd_ref, bwd_ref, rows_ref):
    pick = selector(me_ref[0], parts, steps)
    one = jnp.where(pick, 1.0, 0.0).astype(jnp.bfloat16)
    mixing = mixing_ref[...].astype(jnp.bfloat16)
    same = same_token(pick.shape[0])
    dot = functools.partial(lax.dot_general, preferred_element_type=jnp.float32)
    for ref, dim in ((fwd_ref, 0), (bwd_ref, 1)):
        first = dot(one, mixing, (((1,), (dim,)), ((), ()))).astype(jnp.bfloat16)
        wide = dot(first, one, (((1,), (1,)), ((), ())))
        ref[...] = jnp.where(same, wide, 0.0).astype(jnp.bfloat16)
    thr = jnp.broadcast_to(thr_ref[...], pick.shape)
    rows_ref[...] = jnp.sum(jnp.where(pick, thr, 0.0), axis=1, keepdims=True)


def build_krons(info, mixing, threshold, parts, steps):
    rows = parts * steps * GROUP
    vmem = pl.BlockSpec(memory_space=pltpu.VMEM)
    wide = jax.ShapeDtypeStruct((rows, rows), jnp.bfloat16)
    return pl.pallas_call(
        functools.partial(kron_kernel, parts, steps),
        in_specs=[pl.BlockSpec(memory_space=pltpu.SMEM), vmem, vmem],
        out_specs=(vmem, vmem, vmem),
        out_shape=(wide, wide, jax.ShapeDtypeStruct((rows, 1), jnp.float32)),
        name="build_krons",
    )(info, mixing, threshold.reshape(1, -1))


def rows_of(refs, at, tile):
    return jnp.concatenate([r[:, :, at : at + tile].reshape(-1, tile) for r in refs], axis=0)


def forward_kernel(parts, kron_ref, thr_ref, *refs):
    sources, spikes, surrogate_ref = refs[:parts], refs[parts : 2 * parts], refs[-1]
    steps, group, width = sources[0].shape
    rows = steps * group
    kron = kron_ref[...]
    thr = thr_ref[...]
    tile = 256
    for at in range(0, width, tile):
        cur = rows_of(sources, at, tile)
        shifted = jnp.dot(kron, cur, preferred_element_type=jnp.float32) - thr
        fired = jnp.where(shifted > 0, 1.0, 0.0).astype(jnp.bfloat16)
        for k in range(parts):
            spikes[k][:, :, at : at + tile] = fired[k * rows : (k + 1) * rows].reshape(
                steps, group, tile
            )
        small = jnp.exp(-jnp.abs(shifted))
        part = 1.0 / (1.0 + small)
        surrogate_ref[0, :, at : at + tile] = small * part * part


def forward(kron, thr, sources):
    parts = len(sources)
    steps, tokens, width = sources[0].shape
    piece = pl.BlockSpec((steps, GROUP, width), lambda g: (0, g, 0))
    fixed = lambda shape: pl.BlockSpec(shape, lambda g: (0, 0))
    rows = parts * steps * GROUP
    found = pl.pallas_call(
        functools.partial(forward_kernel, parts),
        grid=(tokens // GROUP,),
        in_specs=[fixed(kron.shape), fixed(thr.shape)] + [piece] * parts,
        out_specs=[piece] * parts + [pl.BlockSpec((1, rows, width), lambda g: (g, 0, 0))],
        out_shape=[jax.ShapeDtypeStruct((steps, tokens, width), jnp.bfloat16)] * parts
        + [jax.ShapeDtypeStruct((tokens // GROUP, rows, width), jnp.float32)],
        name="forward",
    )(kron, thr, *sources)
    return found[:parts], found[parts]


def parts_of(mg):
    high = mg.astype(jnp.bfloat16)
    return high, (mg - high.astype(jnp.float32)).astype(jnp.bfloat16)


def backward_kernel(parts, kron_ref, surrogate_ref, weight_ref, cot_ref, *refs):
    others, outs, last_ref = refs[: parts - 1], refs[parts - 1 : -1], refs[-1]
    steps, group, width = others[0].shape
    rows = steps * group

    @pl.when(pl.program_id(0) == 0)
    def _():
        grad = lax.dot_general(
            cot_ref[...].reshape(-1, width),
            weight_ref[...],
            (((1,), (1,)), ((), ())),
            preferred_element_type=jnp.float32,
        )
        last_ref[...] = grad.astype(jnp.bfloat16).reshape(last_ref.shape)

    here = pl.ds(pl.multiple_of(pl.program_id(0) * group, group), group)
    kron = kron_ref[...]
    tile = 256
    for at in range(0, width, tile):
        spike_grads = [r[:, :, at : at + tile].reshape(rows, tile) for r in others]
        spike_grads.insert(2, last_ref[:, here, at : at + tile].reshape(rows, tile))
        mg = jnp.concatenate(spike_grads, axis=0).astype(jnp.float32)
        mg = mg * surrogate_ref[0, :, at : at + tile]
        grad = jnp.dot(kron, mg.astype(jnp.bfloat16), preferred_element_type=jnp.float32)
        grad = grad.astype(jnp.bfloat16)
        for k in range(parts):
            outs[k][:, :, at : at + tile] = grad[k * rows : (k + 1) * rows].reshape(
                steps, group, tile
            )


def backward(kron, surrogate, weight, cot, others):
    parts = len(others) + 1
    steps, tokens, width = cot.shape
    rows = parts * steps * GROUP
    piece = pl.BlockSpec((steps, GROUP, width), lambda g: (0, g, 0))
    fixed = pl.BlockSpec(cot.shape, lambda g: (0, 0, 0))
    found = pl.pallas_call(
        functools.partial(backward_kernel, parts),
        grid=(tokens // GROUP,),
        in_specs=[
            pl.BlockSpec(kron.shape, lambda g: (0, 0)),
            pl.BlockSpec((1, rows, width), lambda g: (g, 0, 0)),
            pl.BlockSpec(weight.shape, lambda g: (0, 0)),
            fixed,
        ]
        + [piece] * (parts - 1),
        out_specs=[piece] * parts + [fixed],
        out_shape=[jax.ShapeDtypeStruct((steps, tokens, width), jnp.bfloat16)] * (parts + 1),
        cost_estimate=pl.CostEstimate(
            flops=5 * rows * rows * width * (tokens // GROUP),
            bytes_accessed=2 * rows * width * (tokens // GROUP),
            transcendentals=0,
        ),
        name="backward",
    )(kron, surrogate, weight, cot, *others)
    return list(found[:parts]), found[parts]


def cross_of(grads, surrogate, sources, cross_ref, tsum_ref, both_ref):
    width = sources[0].shape[-1]
    every = tsum_ref.shape[0]

    @pl.when(pl.program_id(0) == 0)
    def _():
        cross_ref[...] = jnp.zeros_like(cross_ref)
        tsum_ref[...] = jnp.zeros_like(tsum_ref)

    tile = 256
    total = jnp.zeros((every, 128), jnp.float32)
    for at in range(0, width, tile):
        mg = rows_of(grads, at, tile).astype(jnp.float32) * surrogate(at, tile)
        for piece in range(0, tile, 128):
            total = total + mg[:, piece : piece + 128]
        both_ref[:every, at : at + tile], both_ref[every:, at : at + tile] = parts_of(mg)
    tsum_ref[...] += total
    cross = lax.dot_general(
        both_ref[...],
        rows_of(sources, 0, width),
        (((1,), (1,)), ((), ())),
        preferred_element_type=jnp.float32,
    )
    cross_ref[...] += cross[:every] + cross[every:]


def packed(pick, ours, cross, tsum, out_rows):
    total = pick.shape[1]
    one = jnp.where(pick, 1.0, 0.0)
    left = ours(one)
    exact = functools.partial(
        lax.dot_general, precision=lax.Precision.HIGHEST, preferred_element_type=jnp.float32
    )
    low = lambda dim: jnp.bitwise_and(iota2(cross.shape, dim), GROUP - 1)
    narrow = exact(jnp.where(low(0) == low(1), cross, 0.0), one, (((1,), (0,)), ((), ())))
    weights = exact(left, narrow, (((0,), (0,)), ((), ())))
    row_sum = -jnp.sum(tsum, axis=1, keepdims=True)
    thresholds = jnp.broadcast_to(jnp.sum(left * row_sum, axis=0, keepdims=True), (8, total))
    found = jnp.concatenate([weights, thresholds], axis=0)
    found = jnp.concatenate([found, jnp.zeros((total + 8, 128 - total), jnp.float32)], axis=1)
    return jnp.concatenate([found, jnp.zeros((out_rows - total - 8, 128), jnp.float32)], axis=0)


def early_kernel(parts, info_ref, surrogate_ref, bias_ref, *refs):
    sources, grads, rest = refs[:parts], refs[parts : 2 * parts - 1], refs[2 * parts - 1 :]
    out_ref, cross_ref, tsum_ref, both_ref = rest
    steps = sources[0].shape[0]
    rows = steps * GROUP
    others = lambda value: jnp.concatenate([value[: 2 * rows], value[3 * rows :]], axis=0)
    cross_of(
        grads,
        lambda at, tile: others(surrogate_ref[0, :, at : at + tile]),
        sources,
        cross_ref,
        tsum_ref,
        both_ref,
    )

    @pl.when(pl.program_id(0) == pl.num_programs(0) - 1)
    def _():
        pick = selector(info_ref[0], parts, steps)
        out_ref[...] = packed(pick, others, cross_ref[...], tsum_ref[...], out_ref.shape[0])
        first = pick.shape[1] + 8
        out_ref[first : first + bias_ref.shape[0], :] = bias_ref[...]


def late_kernel(parts, info_ref, surrogate_ref, early_ref, *refs):
    sources, (grad_ref, out_ref, cross_ref, tsum_ref, both_ref) = refs[:parts], refs[parts:]
    steps = grad_ref.shape[0]
    rows = steps * GROUP
    cross_of(
        [grad_ref],
        lambda at, tile: surrogate_ref[0, :, at : at + tile],
        sources,
        cross_ref,
        tsum_ref,
        both_ref,
    )

    @pl.when(pl.program_id(0) == pl.num_programs(0) - 1)
    def _():
        pick = selector(info_ref[0], parts, steps)
        out_ref[...] = early_ref[...] + packed(
            pick,
            lambda value: value[2 * rows : 3 * rows],
            cross_ref[...],
            tsum_ref[...],
            out_ref.shape[0],
        )


def small_sums(info, surrogate, extra, sources, grads):
    parts = len(sources)
    steps, share, width = sources[0].shape
    rows = steps * GROUP
    late = len(grads) == 1
    every = len(grads) * rows
    piece = pl.BlockSpec((steps, GROUP, width), lambda g: (0, g, 0))
    fixed = lambda shape: pl.BlockSpec(shape, lambda g: (0, 0))
    out_rows = extra.shape[0] if late else parts * steps + 8 + -(-extra.shape[0] // 8) * 8
    if late:
        some = pl.BlockSpec((1, rows, width), lambda g: (g, 2, 0))
        cost = pl.CostEstimate(
            flops=8 * parts * parts * rows * rows * width * (share // GROUP),
            bytes_accessed=8 * parts * rows * width * (share // GROUP),
            transcendentals=0,
        )
    else:
        some = pl.BlockSpec((1, parts * rows, width), lambda g: (g, 0, 0))
        cost = SMALL
    return pl.pallas_call(
        functools.partial(late_kernel if late else early_kernel, parts),
        grid=(share // GROUP,),
        in_specs=[SMEM, some, fixed(extra.shape)] + [piece] * (parts + len(grads)),
        out_specs=fixed((out_rows, 128)),
        out_shape=jax.ShapeDtypeStruct((out_rows, 128), jnp.float32),
        scratch_shapes=[
            pltpu.VMEM((every, parts * rows), jnp.float32),
            pltpu.VMEM((every, 128), jnp.float32),
            pltpu.VMEM((2 * every, width), jnp.bfloat16),
        ],
        cost_estimate=cost,
        name="late_sums" if late else "early_sums",
    )(info, surrogate, extra, *sources, *grads)


HBM = pl.BlockSpec(memory_space=pl.ANY)


def place_kernel(slots, info_ref, *refs):
    pieces, (whole_ref, held_ref, in_sems, out_sems) = refs[: len(slots)], refs[len(slots) :]
    share = held_ref.shape[2]
    loads, stores = [], []
    for n, slot in enumerate(slots):
        at = pl.multiple_of(info_ref[slot] * share, share)
        loads.append(pltpu.make_async_copy(pieces[n], held_ref.at[n], in_sems.at[n]))
        stores.append(
            pltpu.make_async_copy(
                held_ref.at[n], whole_ref.at[:, pl.ds(at, share), :], out_sems.at[n]
            )
        )
    for load in loads:
        load.start()
    for load, store in zip(loads, stores):
        load.wait()
        store.start()
    for store in stores:
        store.wait()


def place(info, pieces, slots, tokens):
    steps, share, width = pieces[0].shape
    count = len(pieces)
    return pl.pallas_call(
        functools.partial(place_kernel, tuple(slots)),
        in_specs=[SMEM] + [HBM] * count,
        out_specs=HBM,
        out_shape=jax.ShapeDtypeStruct((steps, tokens, width), jnp.bfloat16),
        scratch_shapes=[
            pltpu.VMEM((count, steps, share, width), jnp.bfloat16),
            pltpu.SemaphoreType.DMA((count,)),
            pltpu.SemaphoreType.DMA((count,)),
        ],
        cost_estimate=SMALL,
        name="place",
    )(info, *pieces)


def combine_kernel(shapes, counts, extra, joined, info_ref, *refs):
    halves = len(shapes)
    keeps, refs = refs[:halves], refs[halves:]
    gots = []
    for count in counts:
        gots.append(refs[:count])
        refs = refs[count:]
    adds, outs = refs[:extra], refs[extra:]
    for h, (before, behind, slot) in enumerate(shapes):
        keep_ref = keeps[h]
        stay_ref, send_ref = (outs[0], outs[1]) if joined else (outs[2 * h], outs[2 * h + 1])
        beta = info_ref[slot]
        each = keep_ref.shape[0] // counts[h]
        cols = slice(h * keep_ref.shape[2], (h + 1) * keep_ref.shape[2]) if joined else slice(None)

        def value(p, b, q):
            at = (p * 2 + b) * behind + q
            if counts[h] == 1:
                got = gots[h][0][at]
            else:
                part = (p * 2 * behind) // each
                got = gots[h][part][at - part * each]
            return keep_ref[at] + got.astype(jnp.float32)

        for p in range(before):
            for q in range(behind):
                stay_ref[p * behind + q, :, cols] = value(p, beta, q)
                send_ref[p * behind + q, :, cols] = value(p, 1 - beta, q).astype(send_ref.dtype)
    if extra:
        total = adds[0][...]
        for ref in adds[1:]:
            total = total + ref[...]
        outs[-1][...] = total


def combine(info, shapes, halves, adds=(), joined=False):
    out = []
    for (keep, _), (before, behind, _) in zip(halves[:1] if joined else halves, shapes):
        cols = keep.shape[2] * (len(halves) if joined else 1)
        shape = (before * behind, keep.shape[1], cols)
        out += [
            jax.ShapeDtypeStruct(shape, jnp.float32),
            jax.ShapeDtypeStruct(shape, jnp.bfloat16),
        ]
    if adds:
        out.append(jax.ShapeDtypeStruct(adds[0].shape, jnp.float32))
    args = [k for k, _ in halves] + [g for _, got in halves for g in got] + list(adds)
    counts = tuple(len(got) for _, got in halves)
    found = pl.pallas_call(
        functools.partial(combine_kernel, tuple(shapes), counts, len(adds), joined),
        in_specs=[SMEM] + [VMEM] * len(args),
        out_specs=[VMEM] * len(out),
        out_shape=out,
        cost_estimate=SMALL,
        name="combine",
    )(info, *args)
    pairs = [(found[n], found[n + 1]) for n in range(0, len(out) - len(out) % 2, 2)]
    return pairs, found[-1]


def final_kernel(total, biases, keep_ref, got_ref, *refs):
    sums_refs, (out_ref, mix_ref, thr_ref, bias_ref) = refs[:-4], refs[-4:]
    out_ref[...] = (keep_ref[...] + got_ref[...].astype(jnp.float32)).astype(jnp.bfloat16)
    sums = sums_refs[0][...]
    for ref in sums_refs[1:]:
        sums = sums + ref[...]
    mix_ref[...] = sums[:total, :total]
    thr_ref[...] = sums[total : total + 1, :total]
    bias_ref[...] = sums[total + 8 : total + 8 + biases]


def final(keep, got, sums, total, width):
    shape = jax.ShapeDtypeStruct
    return pl.pallas_call(
        functools.partial(final_kernel, total, width // 128),
        in_specs=[VMEM] * (2 + len(sums)),
        out_specs=[VMEM] * 4,
        out_shape=[
            shape(keep.shape, jnp.bfloat16),
            shape((total, total), jnp.float32),
            shape((1, total), jnp.float32),
            shape((width // 128, 128), jnp.float32),
        ],
        cost_estimate=SMALL,
        name="final",
    )(keep, got, *sums)


def weight_kernel(shard, parts, info_ref, *refs):
    spikes, cots, outs = refs[:parts], refs[parts : 2 * parts], refs[2 * parts : -1]
    part_ref = refs[-1]
    half = part_ref.shape[1] // 2
    core = jnp.bitwise_and(info_ref[0], 1)
    part_ref[...] = lax.dot_general(
        rows_of(spikes, 0, spikes[0].shape[-1]),
        rows_of(cots, 0, cots[0].shape[-1]),
        (((0,), (0,)), ((), ())),
        preferred_element_type=jnp.float32,
    )
    count = part_ref.shape[0] // shard // 2
    step = pl.program_id(0)
    for side in range(2):
        for n in range(count):
            at = lambda odd: pl.ds(pl.multiple_of((2 * n + odd) * shard, 8), shard)
            cols = slice(side * half, (side + 1) * half)
            outs[side][n] = part_ref[at(core), cols]
            send = part_ref[at(1 - core), cols].astype(jnp.bfloat16)
            for now in range(2):

                @pl.when(step == now)
                def _():
                    outs[2 + 2 * side + now][n] = send


def weight_halves(info, spikes, cots, shard):
    steps, tokens, width = spikes[0].shape
    block, cols = width // 2, width // 2
    count = block // shard // 2
    send = jax.ShapeDtypeStruct((count, shard, cols), jnp.bfloat16)
    keep = jax.ShapeDtypeStruct((2 * count, shard, cols), jnp.float32)
    found = pl.pallas_call(
        functools.partial(weight_kernel, shard, len(spikes)),
        grid=(2,),
        in_specs=[SMEM]
        + [pl.BlockSpec((steps, tokens, block), lambda i: (0, 0, i))] * len(spikes)
        + [pl.BlockSpec((steps, tokens, width), lambda i: (0, 0, 0))] * len(spikes),
        out_specs=[pl.BlockSpec((count, shard, cols), lambda i: (i, 0, 0))] * 2
        + [pl.BlockSpec((count, shard, cols), lambda i: (0, 0, 0))] * 4,
        out_shape=[keep, keep] + [send] * 4,
        scratch_shapes=[pltpu.VMEM((block, width), jnp.float32)],
        cost_estimate=SMALL,
        name="weight_halves",
    )(info, *spikes, *cots)
    return [(found[0], found[2:4]), (found[1], found[4:6])]


def body(ndp, ntm, currents, mixing, threshold, weight, bias, cotangent):
    _, steps, tokens, width = currents.shape
    me = lax.axis_index("tm")
    bits = lambda n: n.bit_length() - 1
    share = tokens // ntm
    bdp, btm = bits(ndp), bits(ntm)
    names = [("dp", b) for b in range(bdp - 1, -1, -1)] + [("tm", b) for b in range(btm - 1, -1, -1)]
    sizes = {"dp": ndp, "tm": ntm}
    info = jnp.stack(
        [me]
        + [(lax.axis_index(axis) >> b) & 1 for axis, b in names]
        + [me ^ k for k in range(ntm)]
    )
    slot = lambda bit: 1 + names.index(bit)
    spot = lambda k: 1 + len(names) + k

    def exchange(pieces):
        return [pieces[0]] + [xor_permute(pieces[k], "tm", ntm, k) for k in range(1, ntm)]

    def cut(value):
        found = {}
        for k in list(range(2, ntm)) + [1, 0]:
            found[k] = lax.dynamic_slice_in_dim(value, (me ^ k) * share, share, axis=1)
            value = after(value, found[k])
        return [found[k] for k in range(ntm)]

    flat = lambda value: value.reshape(-1, width)
    pieces = cut(currents[0])
    currents_in = exchange(pieces)
    cots = exchange(cut(after(cotangent[0], *pieces[1:])))
    kron_fwd, kron_bwd, thr_rows = build_krons(info, mixing, threshold, ntm, steps)

    def spike_grad(cot):
        grad = jnp.einsum("re,de->rd", flat(cot), weight, preferred_element_type=jnp.float32)
        return grad.astype(jnp.bfloat16).reshape(cot.shape)

    bias_term = jnp.sum(flat(cotangent).astype(jnp.float32), axis=0)
    grads = [spike_grad(cot) for cot in cots[:2]]
    spikes, surrogate = forward(kron_fwd, after(thr_rows, bias_term, *grads), currents_in)
    outs = [
        (jnp.dot(flat(spikes[k]), weight, preferred_element_type=jnp.float32) + bias)
        .astype(jnp.bfloat16)
        .reshape(steps, share, width)
        for k in range(ntm)
    ]
    outs_in = exchange(outs)
    grads.append(None)
    grads += [spike_grad(after(cot, *outs)) for cot in cots[3:]]

    others = [k for k in range(ntm) if k != 2]
    early = small_sums(
        info,
        after(surrogate, *outs),
        bias_term.reshape(-1, 128),
        currents_in,
        [grads[k] for k in others],
    )

    shard = width // (ndp * ntm)
    core, y = ("tm", 0), ("dp", 0)
    zs, xs = [("dp", b) for b in range(1, bdp)], [("tm", b) for b in range(1, btm)]
    half = width // 2
    left = names[:-1]

    if shard % 8 == 0:
        late = cots[:2] + [after(cots[2], *outs, early)] + cots[3:]
        halves = weight_halves(info, spikes, late, shard)
    else:
        whole = sum(
            jnp.einsum("rd,re->de", flat(a), flat(b), preferred_element_type=jnp.float32)
            for a, b in zip(spikes, cots)
        ).reshape(-1, 2, shard, width)
        pick = lambda b: lax.dynamic_index_in_dim(whole, b, 1, keepdims=False)
        keep, send = pick(me & 1), pick(1 - (me & 1)).astype(jnp.bfloat16)
        halves = [(keep[..., c : c + half], [send[..., c : c + half]]) for c in (0, half)]

    sent = halves[-1][1][0]
    routes = ([y] + zs[:1], zs[:1] + [y])

    def go(value, *path):
        if all(axis == path[0][0] for axis, _ in path):
            axis = path[0][0]
            return xor_permute(value, axis, sizes[axis], sum(1 << b for _, b in path))
        mask = sum((1 << b) * (ntm if axis == "dp" else 1) for axis, b in path)
        return xor_permute(value, ("dp", "tm"), ndp * ntm, mask)

    def step(state, lefts, bits, joined=False):
        shapes = []
        for rest, bit in zip(lefts, bits):
            p = rest.index(bit)
            shapes.append((1 << p, 1 << (len(rest) - p - 1), slot(bit)))
        pairs, _ = combine(info, shapes, state, (), joined)
        return pairs, [[x for x in rest if x != bit] for rest, bit in zip(lefts, bits)]

    def travel(pairs, bits):
        return [(keep, [go(send, bit)]) for (keep, send), bit in zip(pairs, bits)]

    state = [(keep, [go(after(send, sent), core) for send in sends]) for keep, sends in halves]
    bits = [route[0] for route in routes]
    pairs, lefts = step(state, [left, left], bits)
    state = travel(pairs, bits)
    cgrads, grads[2] = backward(
        kron_bwd,
        surrogate,
        weight,
        after(cots[2], outs_in[-1], *[send for _, send in pairs]),
        [grads[k] for k in others],
    )
    cgrads_in = exchange(cgrads)

    def meet(sums, *bits):
        for bit in bits:
            sums = sums + go(sums, bit)
        return sums

    spots = list(map(spot, range(ntm)))

    def gated(state, *gate):
        return [(after(state[0][0], *gate), state[0][1])] + state[1:]

    bits = [route[1] for route in routes]
    pairs, lefts = step(gated(state, *outs_in[1:3], *cgrads), lefts, bits)
    state = travel(pairs, bits)
    sends = [send for _, send in pairs]
    sums = small_sums(info, after(surrogate, *sends), early, currents_in, grads[2:3])
    hops, gate = [core, y] + zs, [sums, cgrads_in[1]]
    for bit in zs[1:]:
        pairs, lefts = step(gated(state, *gate), lefts, [bit] * len(state), joined=len(state) > 1)
        lefts = lefts[:1]
        state = travel(pairs, [bit])
        sums = after(sums, pairs[0][1])
        if bit == zs[1]:
            sums = meet(sums, core)
            output = place(info, [after(outs_in[0], sums)] + outs_in[1:], spots, tokens)
            sums = meet(after(sums, output) + go(sums, y), hops[2])
            hops = hops[3:]
        else:
            sums, hops = meet(sums, hops[0]), hops[1:]
        gate = [sums]

    pairs, lefts = step(gated(state, *gate), lefts, xs[:1])
    keep, send = pairs[0]
    got = go(send, xs[0])
    current_grad = place(info, [after(cgrads_in[0], send)] + cgrads_in[1:], spots, tokens)
    rest = lefts[0]
    for bit in xs[1:]:
        pairs, (rest,) = step([(keep, [got])], [rest], [bit])
        keep, send = pairs[0]
        got = go(send, bit)
    hops += xs
    sums = after(sums, send)
    sums = [sums] + [
        go(sums, *[bit for i, bit in enumerate(hops) if n >> i & 1])
        for n in range(1, 1 << len(hops))
    ]
    weight_grad, mixing_grad, threshold_grad, bias_grad = final(
        keep.reshape(shard, width), got.reshape(shard, width), sums, ntm * steps, width
    )
    return (
        output[None],
        current_grad[None],
        weight_grad,
        mixing_grad,
        threshold_grad.reshape(-1),
        bias_grad.reshape(-1),
    )


def solution(mesh):
    return jax.shard_map(
        functools.partial(body, mesh.shape["dp"], mesh.shape["tm"]),
        mesh=mesh,
        in_specs=(P("dp", "tm", None, None), P(), P(), P(), P(), P("dp", "tm", None, None)),
        out_specs=(
            P("dp", "tm", None, None),
            P("dp", "tm", None, None),
            P(("dp", "tm"), None),
            P(),
            P(),
            P(),
        ),
        check_vma=False,
    )
```
